512 devices in a mesh: section: 8 (over x, core), expert: 64 (over z, y).
Axes of the slice: x: 4, y: 8, z: 8, core: 2. Of those that a mesh axis runs over, the one named last changes fastest.
Arguments:
- histories: bfloat16 [8, 8192, 5120], P('section', 'expert'), may hold values from -6 to 6
- page_map: int32 [8, 2, 2048], P('section', None, 'expert'), may hold values from 0 to 2047, as said below
- user_pages: int32 [8, 64, 4], P('section', 'expert'), may hold values from 1 to 16, 32 in all within a row
- tails: int32 [8, 64, 4], P('section', 'expert'), may hold values from 1 to 4
- routes: int32 [8, 8192, 2], P('section', 'expert'), may hold values from 0 to 31, all different within a row; in each aligned block of 128 rows (0 to 127, 128 to 255, ..., all dimensions but the last counted through in order) at most 16 rows name the same one
- out_proj: bfloat16 [8, 1024, 1024], P('section', 'expert'), may hold values from -0.1875 to 0.1875
- router: bfloat16 [8, 1024, 32], P('section'), may hold values from -0.75 to 0.75
- w_gate: bfloat16 [8, 1024, 32768], P('section', None, 'expert'), may hold values from -0.1875 to 0.1875
- w_up: bfloat16 [8, 1024, 32768], P('section', None, 'expert'), may hold values from -0.1875 to 0.1875
- w_down: bfloat16 [8, 32768, 1024], P('section', 'expert'), may hold values from -0.1875 to 0.1875
Outputs:
- handed: bfloat16 [8, 8192, 1024], P('section', 'expert')
The draws below stay inside these ranges and needn't reach their ends.
Inputs may be any that keep to these rules, and one draw needn't show every extreme that they name: page_map[0] is a permutation of the pages of a section and page_map[1] its inverse; every device holds exactly 32 pages before and after; no device's pages send more than 1 pages to one device, and some send exactly 1. `user_pages`: the 4 entries of one device sum to 32, and the largest is 16. `routes`: A row names 2 different experts; among the rows of one device, no expert is named more than 16 times, a bound that some block reaches.
All inputs are finite; a program needn't handle non-finite values.
Results may differ from the reference program's by a relative error of at most 0.012.
Values may be sent and summed in bfloat16 or wider, within the bound.
No kernel may reach another device: no remote copies, remote signals or barrier semaphores. Data moves between devices by JAX's collectives and lax.ppermute only.
A program may use at most 64 MiB of HBM per device.

```python
import math
import jax
import jax.numpy as jnp
import numpy as np
from jax import lax

D = 1024
HEADS = 8
HID = 1024
EXPERTS = 32
TOP = 2
PAGE = 4
PAGES_DEV = 32
USERS_DEV = 4
MAXPAGES = 16
TOK_DEV = 128
TOKENS = 8192
NPAGES = 2048
SECTIONS = 8
CAP = 16
N_EXPERT = 64


def section_pages(section_key):
    device_count = N_EXPERT
    first_key, second_key, third_key, fourth_key, fifth_key = jax.random.split(section_key, 5)
    place_perm = jax.random.permutation(first_key, device_count).astype(jnp.int32)
    shift_perm = jax.random.permutation(second_key, device_count).astype(jnp.int32)
    offset_perm = jax.random.permutation(third_key, device_count).astype(jnp.int32)
    page_index = jnp.arange(PAGES_DEV, dtype=jnp.int32)
    offsets = offset_perm[page_index % device_count]
    sender = jnp.arange(device_count, dtype=jnp.int32)
    receiver = place_perm[(shift_perm[:, None] + offsets[None, :]) % device_count]
    arrival_perm = jax.vmap(lambda sub_key: jax.random.permutation(sub_key, PAGES_DEV))(jax.random.split(fourth_key, device_count)).astype(jnp.int32)
    holding_perm = jax.vmap(lambda sub_key: jax.random.permutation(sub_key, PAGES_DEV))(jax.random.split(fifth_key, device_count)).astype(jnp.int32)
    arrival_slot = arrival_perm[receiver, page_index[None, :]]
    global_target = (receiver * PAGES_DEV + arrival_slot).reshape(-1).astype(jnp.int32)
    global_source = (sender[:, None] * PAGES_DEV + holding_perm).reshape(-1).astype(jnp.int32)
    forward = jnp.zeros((NPAGES,), jnp.int32).at[global_source].set(global_target)
    inverse = jnp.zeros((NPAGES,), jnp.int32).at[global_target].set(global_source)
    return jnp.stack([forward, inverse])


def draw_page_map(key, part):
    return jax.vmap(section_pages)(jax.random.split(jax.random.fold_in(key, 11), SECTIONS))


def plant(entries, stream_key, low, high):
    place = [jax.random.randint(jax.random.fold_in(stream_key, axis), (), 0, length) for axis, length in enumerate(entries.shape)]
    main_axis = entries.shape.index(max(entries.shape))
    next_to = place[:main_axis] + [(place[main_axis] + 1) % entries.shape[main_axis]] + place[main_axis + 1:]
    return entries.at[tuple(place)].set(low).at[tuple(next_to)].set(high)


def levels(key, extent, shards, least, largest):
    loudness, own = 1.0, jax.random.fold_in(key, 6)
    for axis_at, shards_of in shards:
        draws = jnp.exp(jax.random.uniform(jax.random.fold_in(own, axis_at), (shards_of,), jnp.float32, least / len(shards), largest / len(shards)))
        loudness = loudness * jnp.repeat(draws, extent[axis_at] // shards_of).reshape([-1 if axis == axis_at else 1 for axis in range(len(extent))])
    return loudness


def length_profile(amount, total, most, slope):
    weights = [(1 << 20) // math.isqrt(standing ** slope) + 1 for standing in range(2, amount + 1)]
    spare, given = total - most - (amount - 1), [1] * (amount - 1)
    while spare > 0:
        movable = [i for i in range(amount - 1) if given[i] < most]
        mass, remaining = sum([weights[i] for i in movable]), spare
        for i in movable:
            addition = min(most - given[i], max(1, remaining * weights[i] // mass), spare)
            given[i] = given[i] + addition
            spare = spare - addition
    return np.array([most] + given)


def ragged_sizes(rng, number_of, total, bound, lean):
    if number_of == 2:
        one = jax.random.randint(rng, (), max(1, total - bound), min(bound, total - 1) + 1)
        return jnp.stack([one, total - one])
    lengths = jnp.asarray(length_profile(number_of, total, bound, lean), jnp.int32)
    twos = (number_of - 1) // 2
    source_of, taker = lengths[1:1 + 2 * twos:2], lengths[2:2 + 2 * twos:2]
    margin = jnp.minimum(source_of - 1, bound - taker)
    moved = jax.random.randint(jax.random.fold_in(rng, 1), (twos,), 0, 1 << 20) % (margin + 1)
    lengths = lengths.at[1:1 + 2 * twos:2].set(source_of - moved).at[2:2 + 2 * twos:2].set(taker + moved)
    return lengths[jax.random.permutation(jax.random.fold_in(rng, 2), number_of)]


def shared_out(key, own, number, rows, number_of, top, most, skew):
    order = jax.random.permutation(key, number_of)
    heavy_load, ordinary = load_shares(number_of, rows * top, most, skew, True), load_shares(number_of, rows * top, most, skew, False)
    places = jnp.arange(number_of)

    def named(sizes, turn):
        used = int((sizes > 0).sum())
        fixed = max(1, used // 4)
        passed = fixed + (places - fixed + turn * (used - fixed)) % max(1, number_of - fixed)
        return jnp.zeros((number_of,), jnp.int32).at[order[jnp.where(places < fixed, places, passed)]].set(jnp.asarray(sizes, jnp.int32))

    sizes = jnp.where(number % 4 == 0, named(heavy_load, number // 4), named(ordinary, number - number // 4 - 1))
    mixed = jax.random.permutation(jax.random.fold_in(own, 3), number_of)
    donor, taker = mixed[0:number_of // 2 * 2:2], mixed[1:number_of // 2 * 2:2]
    room = jnp.minimum(sizes[donor] - 1, most - sizes[taker]) // 2
    room = jnp.where((donor == order[0]) | (taker == order[0]) | (sizes[taker] == 0), 0, jnp.maximum(room, 0))
    passed = jax.random.randint(jax.random.fold_in(own, 4), (number_of // 2,), 0, 1 << 20) % (room + 1)
    sizes = sizes.at[donor].add(-passed).at[taker].add(passed)
    items = jnp.searchsorted(jnp.cumsum(sizes), jnp.arange(rows * top), side="right").astype(jnp.int32)
    grid = items.reshape(top, rows).T
    grid = grid[jax.random.permutation(jax.random.fold_in(own, 1), rows)]
    turn = jax.random.randint(jax.random.fold_in(own, 2), (rows, 1), 0, top)
    return jnp.take_along_axis(grid, (jnp.arange(top)[None, :] + turn) % top, axis=1)


def load_shares(amount, total, limit, slope, full):
    portions = [(1 << 20) // math.isqrt(standing ** slope) + 1 for standing in range(1, amount + 1)]
    largest = limit if full else min(limit, max(-(-total // amount), total * portions[0] // sum(portions)))
    least = 1 if total - largest >= amount - 1 else 0
    holding, rest = [largest] + [least] * (amount - 1), total - largest - least * (amount - 1)
    while rest > 0:
        free = [i for i in range(1, amount) if holding[i] < largest] or [i for i in range(1, amount) if holding[i] < limit]
        whole, remaining = sum([portions[i] for i in free]), rest
        for i in free:
            extra = min(limit - holding[i], max(1, remaining * portions[i] // whole), rest)
            holding[i] = holding[i] + extra
            rest = rest - extra
    return np.array(holding)


def normal_values(own_key, extent, scale, limit, pieces=(), held_as=jnp.bfloat16):
    level = levels(own_key, extent, pieces, -0.22, 0.18) if pieces else 1.0
    values = jax.random.normal(own_key, extent, jnp.float32) * scale * level
    return jnp.minimum(jnp.maximum(values, -limit), limit).astype(held_as)


def setup_inputs(seed: int = 0) -> dict:
    streams_of = jax.random.split(jax.random.key(seed), 11)
    histories = normal_values(streams_of[0], (SECTIONS, TOKENS, 5 * D), 1.0, 6.0, ((0, 8), (1, 64)))
    page_map = draw_page_map(jax.random.fold_in(streams_of[10], 71), 0)
    user_pages = jax.vmap(lambda own: ragged_sizes(own, USERS_DEV, PAGES_DEV, MAXPAGES, 2))(jax.random.split(streams_of[2], SECTIONS * N_EXPERT)).reshape((SECTIONS, N_EXPERT, USERS_DEV)).astype(jnp.int32)
    tails = plant(jax.random.randint(streams_of[3], (SECTIONS, N_EXPERT, USERS_DEV), 1, PAGE + 1), jax.random.fold_in(streams_of[3], 1), 1, PAGE).astype(jnp.int32)
    routes_keys = jax.random.split(jax.random.fold_in(streams_of[4], 1), SECTIONS * TOKENS // TOK_DEV)
    routes_turns = jax.random.permutation(jax.random.fold_in(streams_of[4], 3), SECTIONS * TOKENS // TOK_DEV)
    routes = jax.vmap(lambda own, number: shared_out(jax.random.fold_in(streams_of[4], 2), own, number, TOK_DEV, EXPERTS, TOP, CAP, 2))(routes_keys, routes_turns).reshape((SECTIONS, TOKENS, TOP))
    out_proj = normal_values(streams_of[5], (SECTIONS, D, D), D ** -0.5, 0.1875, ((0, 8), (1, 64)))
    router = normal_values(streams_of[6], (SECTIONS, D, EXPERTS), (D // 16) ** -0.5, 0.75, ((0, 8),))
    w_gate = normal_values(streams_of[7], (SECTIONS, D, EXPERTS * HID), D ** -0.5, 0.1875, ((0, 8), (2, 64)))
    w_up = normal_values(streams_of[8], (SECTIONS, D, EXPERTS * HID), D ** -0.5, 0.1875, ((0, 8), (2, 64)))
    w_down = normal_values(streams_of[9], (SECTIONS, EXPERTS * HID, D), HID ** -0.5, 0.1875, ((0, 8), (1, 64)))
    return dict(histories=histories, page_map=page_map, user_pages=user_pages, tails=tails, routes=routes, out_proj=out_proj, router=router, w_gate=w_gate, w_up=w_up, w_down=w_down)


def layout_rows(counts, tail_rows, page_rows, row_count):
    counts = counts.astype(jnp.int32)
    starting = (jnp.cumsum(counts) - counts).astype(jnp.int32)
    length = ((counts - 1) * page_rows + tail_rows).astype(jnp.int32)
    row_index = jnp.arange(row_count, dtype=jnp.int32)
    page_of = row_index // page_rows
    owner_of = lax.optimization_barrier(jnp.sum((starting[None, :] <= page_of[:, None]).astype(jnp.int32), axis=1)) - 1
    member = owner_of[:, None] == jnp.arange(counts.shape[0], dtype=jnp.int32)[None, :]
    offset = lax.optimization_barrier(jnp.sum(jnp.where(member, starting[None, :] * page_rows, 0), axis=1))
    spread = lax.optimization_barrier(jnp.sum(jnp.where(member, length[None, :], 0), axis=1))
    return (owner_of, row_index - offset, spread)

def attend(balanced, counts, tail_rows):
    row_count = balanced.shape[0]
    model_width = balanced.shape[1] // 5
    head_dim = model_width // HEADS
    owner_of, position, spread = layout_rows(counts, tail_rows, PAGE, row_count)
    allowed = (owner_of[:, None] == owner_of[None, :]) & (position[None, :] <= position[:, None]) & (position[None, :] < spread[None, :])
    queries = balanced[:, :model_width].reshape(row_count, HEADS, head_dim).astype(jnp.float32)
    key_rows = balanced[:, model_width:2 * model_width].reshape(row_count, HEADS, head_dim).astype(jnp.float32)
    values = balanced[:, 2 * model_width:3 * model_width].reshape(row_count, HEADS, head_dim)
    scores = jnp.einsum('qhd,khd->hqk', queries, key_rows) * head_dim ** (-0.5)
    weights = jnp.where(allowed[None], jax.nn.silu(scores), 0.0) / spread.astype(jnp.float32)[None, :, None]
    weights = weights.astype(jnp.bfloat16)
    attended = jnp.einsum('hqk,khd->qhd', weights.astype(jnp.float32), values.astype(jnp.float32)).reshape(row_count, model_width)
    average = lax.optimization_barrier(jnp.mean(attended, axis=1, keepdims=True))
    centered = attended - average
    variance = lax.optimization_barrier(jnp.mean(centered * centered, axis=1, keepdims=True))
    gating = balanced[:, 3 * model_width:4 * model_width].astype(jnp.float32)
    return (centered * lax.rsqrt(variance + 1e-05) * gating).astype(jnp.bfloat16)

def gate_share(normed, router, routes):
    logits = jnp.dot(normed, router, preferred_element_type=jnp.float32)
    scores = jax.nn.sigmoid(logits)
    picked = routes[:, :, None] == jnp.arange(router.shape[1], dtype=jnp.int32)[None, None, :]
    chosen = lax.optimization_barrier(jnp.sum(jnp.where(picked, scores[:, None, :], 0.0), axis=2))
    return chosen / lax.optimization_barrier(jnp.sum(chosen, axis=1, keepdims=True))

def slot_table(routes, experts, capacity):
    pair_count = routes.shape[0] * routes.shape[1]
    chosen = routes.reshape(-1).astype(jnp.int32)
    onehot = (chosen[:, None] == jnp.arange(experts, dtype=jnp.int32)[None, :]).astype(jnp.int32)
    before = jnp.cumsum(onehot, axis=0) - onehot
    ranking = lax.optimization_barrier(jnp.sum(before * onehot, axis=1)).astype(jnp.int32)
    slot_of_pair = chosen * capacity + ranking
    matches = slot_of_pair[None, :] == jnp.arange(experts * capacity, dtype=jnp.int32)[:, None]
    source_token = lax.optimization_barrier(jnp.sum(jnp.where(matches, jnp.arange(pair_count, dtype=jnp.int32)[None, :], 0), axis=1)) // 2
    return (slot_of_pair, source_token.astype(jnp.int32))

def expert_ffn(flat_rows, gate_cols, up_cols, down_rows):
    gate_act = jnp.dot(flat_rows, gate_cols, preferred_element_type=jnp.float32)
    up_act = jnp.dot(flat_rows, up_cols, preferred_element_type=jnp.float32)
    hidden = (jax.nn.silu(gate_act) * up_act).astype(jnp.bfloat16)
    half_units = HID // 2
    first_part = jnp.dot(hidden[:, :half_units], down_rows[:half_units], preferred_element_type=jnp.float32).astype(jnp.bfloat16)
    second_part = jnp.dot(hidden[:, half_units:], down_rows[half_units:], preferred_element_type=jnp.float32).astype(jnp.bfloat16)
    return (first_part.astype(jnp.float32) + second_part.astype(jnp.float32)).astype(jnp.bfloat16)

def one_section(histories, page_map, user_pages, tails, routes, out_proj, router, w_gate, w_up, w_down):
    page_block = histories.reshape(NPAGES, PAGE, 5 * D)
    placed = jnp.zeros_like(page_block).at[page_map[0].astype(jnp.int32)].set(page_block)
    balanced = placed.reshape(N_EXPERT, TOK_DEV, 5 * D)
    mixed_in = lax.map(lambda item_pack: attend(item_pack[0], item_pack[1], item_pack[2]), (balanced, user_pages, tails))
    mixed_in = mixed_in.reshape(TOKENS, D)
    flat_rows = balanced.reshape(TOKENS, 5 * D)
    resid = (flat_rows[:, 4 * D:].astype(jnp.float32) + jnp.dot(mixed_in, out_proj, preferred_element_type=jnp.float32)).astype(jnp.bfloat16)
    resid_wide = resid.astype(jnp.float32)
    normed = (resid_wide * lax.rsqrt(lax.optimization_barrier(jnp.mean(resid_wide * resid_wide, axis=1, keepdims=True)) + 1e-06)).astype(jnp.bfloat16)
    share = gate_share(normed, router, routes)
    slot_of_pair, source_token = jax.vmap(lambda group: slot_table(group, EXPERTS, CAP))(routes.reshape(N_EXPERT, TOK_DEV, 2))
    token_ids = source_token + (jnp.arange(N_EXPERT, dtype=jnp.int32) * TOK_DEV)[:, None]
    table = token_ids.reshape(N_EXPERT, EXPERTS, CAP).transpose(1, 0, 2).reshape(EXPERTS, N_EXPERT * CAP)
    gate_all = w_gate.reshape(D, EXPERTS, HID).transpose(1, 0, 2)
    up_all = w_up.reshape(D, EXPERTS, HID).transpose(1, 0, 2)
    down_all = w_down.reshape(EXPERTS, HID, D)
    outputs = lax.map(lambda item_pack: expert_ffn(normed[item_pack[0]], item_pack[1], item_pack[2], item_pack[3]), (table, gate_all, up_all, down_all))
    outputs = outputs.reshape(EXPERTS, N_EXPERT, CAP, D).transpose(1, 0, 2, 3).reshape(N_EXPERT, EXPERTS * CAP, D)
    picked = jax.vmap(lambda block_out, block_slot: block_out[block_slot])(outputs, slot_of_pair)
    picked = picked.reshape(TOKENS, 2, D).astype(jnp.float32)
    mixture = lax.optimization_barrier(jnp.sum(picked * share[:, :, None], axis=1))
    return (resid_wide + mixture).astype(jnp.bfloat16)

def reference(histories, page_map, user_pages, tails, routes, out_proj, router, w_gate, w_up, w_down):
    results = []
    for section_index in range(SECTIONS):
        results.append(one_section(histories[section_index], page_map[section_index], user_pages[section_index], tails[section_index], routes[section_index], out_proj[section_index], router[section_index], w_gate[section_index], w_up[section_index], w_down[section_index]))
    output_rows = jnp.stack(results)
    return jnp.roll(output_rows, 1, axis=0)
```

```python
import functools

import jax
import jax.numpy as jnp
from jax import lax
from jax.experimental import pallas as pl
from jax.experimental.pallas import tpu as pltpu
from jax.sharding import PartitionSpec as P


HEADS = 8
SIDE = 8
F32 = jnp.float32
BF16 = jnp.bfloat16
VMEM = pltpu.VMEM
SMEM = pltpu.SMEM


def iota(shape, axis):
    return lax.broadcasted_iota(jnp.int32, shape, axis)


def dot(a, b):
    return jnp.dot(a, b, preferred_element_type=F32)


def dot_t(a, b):
    return lax.dot_general(a, b, (((1,), (1,)), ((), ())), preferred_element_type=F32)


def flag(mask):
    return jnp.where(mask, 1.0, 0.0).astype(BF16)


def whole(space=VMEM):
    return pl.BlockSpec(memory_space=space)


def pack_pages_body(map_ref, rows_ref, out_ref, pick_ref):
    @pl.when(pl.program_id(0) == 0)
    def _():
        device = lax.shift_right_logical(map_ref[0, 0:1, :], 5).astype(F32)
        pages = device.shape[1]
        rows = pages * 4
        spread = flag(iota((pages, rows), 0) == lax.shift_right_logical(iota((pages, rows), 1), 2))
        target = dot(jnp.broadcast_to(device, (8, pages)).astype(BF16), spread)[0:1]
        slot = iota((pick_ref.shape[0], rows), 0)
        row = iota((pick_ref.shape[0], rows), 1)
        hit = (lax.shift_right_logical(slot, 3) == target.astype(jnp.int32)) & ((slot & 3) == (row & 3))
        pick_ref[:, :rows] = flag(hit & ((slot & 4) == 0))
        pick_ref[:, rows:] = flag(hit & ((slot & 4) == 4))

    half = rows_ref.shape[1] // 2
    both = jnp.concatenate([rows_ref[:, :half], rows_ref[:, half:]], axis=0)
    out_ref[...] = dot(pick_ref[...], both).astype(BF16)


def pack_pages(page_map, rows, devices):
    count, width = rows.shape
    block = width // 5
    slots = devices * 8
    return pl.pallas_call(
        pack_pages_body,
        name="pack_pages",
        grid=(5,),
        in_specs=[
            whole(),
            pl.BlockSpec((count, block), lambda b: (0, b)),
        ],
        out_specs=pl.BlockSpec((slots, block // 2), lambda b: (0, b)),
        out_shape=jax.ShapeDtypeStruct((slots, width // 2), BF16),
        scratch_shapes=[pltpu.VMEM((slots, 2 * count), BF16)],
        cost_estimate=pl.CostEstimate(flops=1 << 30, bytes_accessed=4 << 20, transcendentals=0),
    )(page_map, rows)


def user_layout(index, pages_ref, tails_ref):
    users = pages_ref.shape[2]
    owner = jnp.zeros_like(index)
    offset = jnp.zeros_like(index)
    length = jnp.zeros_like(index) + ((pages_ref[0, 0, 0] - 1) * 4 + tails_ref[0, 0, 0])
    start = 0
    for user in range(1, users):
        start = start + pages_ref[0, 0, user - 1] * 4
        inside = index >= start
        owner = jnp.where(inside, user, owner)
        offset = jnp.where(inside, start, offset)
        length = jnp.where(inside, (pages_ref[0, 0, user] - 1) * 4 + tails_ref[0, 0, user], length)
    return owner, offset, length


def token_body(
    place_ref, pages_ref, tails_ref, map_ref, routes_ref, arrived_ref, router_ref, *refs
):
    proj_refs = refs[:SIDE]
    normed_ref, resid_ref, share_ref, mixed_ref = refs[SIDE:]
    count = resid_ref.shape[0]
    slots = arrived_ref.shape[0]
    half = arrived_ref.shape[1] // 5
    pages = map_ref.shape[2]
    model_width = 2 * half
    head_dim = model_width // HEADS

    source = lax.shift_right_logical(map_ref[0, 1:2, :], 5).astype(F32)
    mine = lax.shift_right_logical(iota((count, pages), 0), 2) == iota((count, pages), 1)
    source = jnp.sum(jnp.where(mine, source, 0.0), axis=1, keepdims=True).astype(jnp.int32)
    slot = iota((count, slots), 1)
    near = lax.shift_right_logical(slot, 3) == source
    row = iota((count, slots), 0) & 3
    picks = [flag(near & ((slot & 7) == row + 4 * side)) for side in range(2)]

    def block(index, side):
        return dot(picks[side], arrived_ref[:, index * half : (index + 1) * half])

    rows = iota((count, count), 0)
    keys = iota((count, count), 1)
    row_owner, _, row_length = user_layout(rows, pages_ref, tails_ref)
    key_owner, key_offset, key_length = user_layout(keys, pages_ref, tails_ref)
    allowed = (row_owner == key_owner) & (keys <= rows) & (keys - key_offset < key_length)
    factor = jnp.where(allowed, 1.0 / row_length.astype(F32), 0.0)
    attended = []
    for side in range(2):
        queries = block(0, side).astype(BF16)
        key_rows = block(1, side).astype(BF16)
        values = block(2, side).astype(BF16)
        for head in range(HEADS // 2):
            part = slice(head * head_dim, (head + 1) * head_dim)
            scores = dot_t(queries[:, part], key_rows[:, part]) * head_dim ** (-0.5)
            weights = (scores * jax.nn.sigmoid(scores) * factor).astype(BF16)
            attended.append(dot(weights, values[:, part]))
    total = functools.reduce(jnp.add, attended)
    average = jnp.sum(total, axis=1, keepdims=True) * (1.0 / model_width)
    attended = [part - average for part in attended]
    squares = functools.reduce(jnp.add, [part * part for part in attended])
    variance = jnp.sum(squares, axis=1, keepdims=True) * (1.0 / model_width)
    scale = lax.rsqrt(variance + 1e-05)
    for side in range(2):
        gating = block(3, side)
        for head in range(HEADS // 2):
            part = slice(head * head_dim, (head + 1) * head_dim)
            index = side * (HEADS // 2) + head
            mixed_ref[index] = (attended[index] * scale * gating[:, part]).astype(BF16)

    place = place_ref[0]
    order = [0, 1, 2, 3, 4, -1, -2, -3]
    mixed = [mixed_ref[(place - shift) & (SIDE - 1)] for shift in order]
    squares = jnp.zeros((count, 1), F32)
    chunk = half // 2
    for side in range(2):
        inputs = block(4, side)
        for quarter in range(2):
            part = slice(side * half + quarter * chunk, side * half + (quarter + 1) * chunk)
            projected = dot(mixed[0], proj_refs[0][:, part])
            for index in range(1, SIDE):
                projected += dot(mixed[index], proj_refs[index][:, part])
            resid = (inputs[:, quarter * chunk : (quarter + 1) * chunk] + projected).astype(BF16)
            resid_ref[:, part] = resid
            wide = resid.astype(F32)
            squares += jnp.sum(wide * wide, axis=1, keepdims=True)
    scale = lax.rsqrt(squares * (1.0 / model_width) + 1e-06)
    for quarter in range(4):
        part = slice(quarter * chunk, (quarter + 1) * chunk)
        normed_ref[:, part] = (resid_ref[:, part].astype(F32) * scale).astype(BF16)

    experts = router_ref.shape[0]
    scores = jax.nn.sigmoid(dot_t(router_ref[...], normed_ref[...]))
    expert = iota((experts, count), 0)
    chosen = [
        jnp.sum(jnp.where(expert == routes_ref[k : k + 1, :], scores, 0.0), axis=0, keepdims=True)
        for k in range(2)
    ]
    share_ref[...] = jnp.zeros(share_ref.shape, F32)
    for k in range(2):
        share_ref[k : k + 1, :] = chosen[k] / (chosen[0] + chosen[1])


def token_stage(place, user_pages, tails, page_map, routes, arrived, router, proj, count):
    width = arrived.shape[1] // 5 * 2
    return pl.pallas_call(
        token_body,
        name="token_stage",
        in_specs=[whole(SMEM)] * 3 + [whole()] * (4 + SIDE),
        out_specs=[whole()] * 3,
        out_shape=[
            jax.ShapeDtypeStruct((count, width), BF16),
            jax.ShapeDtypeStruct((count, width), BF16),
            jax.ShapeDtypeStruct((8, count), F32),
        ],
        scratch_shapes=[pltpu.VMEM((HEADS, count, width // HEADS), BF16)],
        cost_estimate=pl.CostEstimate(flops=2 << 30, bytes_accessed=6 << 20, transcendentals=0),
    )(place, user_pages, tails, page_map, routes, arrived, router, *proj)


def slots_body(experts, core_ref, mine_ref, theirs_ref, pick_ref, lanes_ref):
    count = mine_ref.shape[1]
    core = core_ref[0]
    capacity = 4 * count // experts
    expert = iota((experts, count), 0)
    earlier = flag(iota((count, count), 0) < iota((count, count), 1))
    row = iota((pick_ref.shape[0], count), 0)
    lanes_ref[...] = jnp.zeros(lanes_ref.shape, F32)
    for side, routes_ref in enumerate((mine_ref, theirs_ref)):
        chosen = [routes_ref[k : k + 1, :] for k in range(2)]
        named = [expert == chosen[k] for k in range(2)]
        before = dot(flag(named[0] | named[1]), earlier)
        lanes = []
        for k in range(2):
            rank = jnp.sum(jnp.where(named[k], before, 0.0), axis=0, keepdims=True)
            slot = chosen[k] * capacity + rank.astype(jnp.int32)
            half = lax.shift_right_logical(slot, 3) & 1
            lanes.append(jnp.where(half == core, slot ^ (8 * side), -1))
            lanes_ref[2 * side + k : 2 * side + k + 1, :] = lanes[k].astype(F32)
        pick_ref[:, side * count : (side + 1) * count] = flag((row == lanes[0]) | (row == lanes[1]))


def slot_tables(core, mine, theirs, experts):
    count = mine.shape[1]
    rows = 4 * count
    return pl.pallas_call(
        functools.partial(slots_body, experts),
        name="slot_tables",
        in_specs=[whole(SMEM), whole(), whole()],
        out_specs=[whole()] * 2,
        out_shape=[
            jax.ShapeDtypeStruct((rows, 2 * count), BF16),
            jax.ShapeDtypeStruct((8, count), F32),
        ],
        cost_estimate=pl.CostEstimate(flops=1 << 24, bytes_accessed=1 << 18, transcendentals=0),
    )(core, mine, theirs)


def pack_rows_body(pick_ref, mine_ref, theirs_ref, out_ref):
    _, width = mine_ref.shape
    chunk = width // 4
    for quarter in range(4):
        part = slice(quarter * chunk, (quarter + 1) * chunk)
        rows = jnp.concatenate([mine_ref[:, part], theirs_ref[:, part]], axis=0)
        out_ref[:, part] = dot(pick_ref[...], rows).astype(BF16)


def pack_rows(pick, mine, theirs):
    return pl.pallas_call(
        pack_rows_body,
        name="pack_rows",
        in_specs=[whole()] * 3,
        out_specs=whole(),
        out_shape=jax.ShapeDtypeStruct((pick.shape[0], mine.shape[1]), BF16),
        cost_estimate=pl.CostEstimate(flops=1 << 28, bytes_accessed=2 << 20, transcendentals=0),
    )(pick, mine, theirs)


def expert_body(added, rows_ref, gate_ref, up_ref, down_ref, *refs):
    out_ref, total_ref = refs[-2:]
    step = pl.program_id(0)
    tile = 256
    for index in range(rows_ref.shape[0] // tile):
        part = slice(index * tile, (index + 1) * tile)
        rows = rows_ref[part, :]
        gate = dot(rows, gate_ref[...])
        hidden = (gate * jax.nn.sigmoid(gate) * dot(rows, up_ref[...])).astype(BF16)
        result = dot(hidden, down_ref[...])

        @pl.when(step == 0)
        def _():
            total_ref[part, :] = result

        @pl.when(step == 1)
        def _():
            half = (total_ref[part, :] + result).astype(BF16)
            if added:
                half = (half.astype(F32) + refs[0][part, :].astype(F32)).astype(BF16)
            out_ref[part, :] = half


def expert_half(rows, gate, up, down, earlier=None):
    count, width = rows.shape
    chunk = gate.shape[1] // 2
    added = earlier is not None
    extra = (earlier,) if added else ()
    return pl.pallas_call(
        functools.partial(expert_body, added),
        name="expert_half",
        grid=(2,),
        in_specs=[
            pl.BlockSpec((count, width), lambda c: (0, 0)),
            pl.BlockSpec((width, chunk), lambda c: (0, c)),
            pl.BlockSpec((width, chunk), lambda c: (0, c)),
            pl.BlockSpec((chunk, width), lambda c: (c, 0)),
        ]
        + [pl.BlockSpec((count, width), lambda c: (0, 0))] * len(extra),
        out_specs=pl.BlockSpec((count, width), lambda c: (0, 0)),
        out_shape=jax.ShapeDtypeStruct((count, width), BF16),
        scratch_shapes=[pltpu.VMEM((count, width), F32)],
        cost_estimate=pl.CostEstimate(flops=2 << 30, bytes_accessed=5 << 20, transcendentals=0),
    )(rows, gate, up, down, *extra)


def combine_body(lanes_ref, mine_ref, theirs_ref, resid_ref, rows_ref, own_ref, other_ref):
    count, width = resid_ref.shape
    slots = rows_ref.shape[0]
    table = jnp.concatenate([lanes_ref[0:4, :], mine_ref[0:2, :], theirs_ref[0:2, :]], axis=0)
    table = jnp.transpose(table)
    slot = iota((count, slots), 1).astype(F32)
    shares = []
    for side in range(2):
        share = jnp.zeros((count, slots), F32)
        for k in range(2):
            lane = 2 * side + k
            share += jnp.where(slot == table[:, lane : lane + 1], table[:, 4 + lane : 5 + lane], 0.0)
        high = share.astype(BF16)
        shares.append((high, (share - high.astype(F32)).astype(BF16)))
    chunk = width // 4
    for quarter in range(4):
        part = slice(quarter * chunk, (quarter + 1) * chunk)
        rows = rows_ref[:, part]
        own, other = [dot(high, rows) + dot(low, rows) for high, low in shares]
        own_ref[:, part] = (resid_ref[:, part].astype(F32) + own).astype(BF16)
        other_ref[:, part] = other.astype(BF16)


def combine(lanes, mine, theirs, resid, rows):
    return pl.pallas_call(
        combine_body,
        name="combine",
        in_specs=[whole()] * 5,
        out_specs=[whole()] * 2,
        out_shape=[jax.ShapeDtypeStruct(resid.shape, BF16)] * 2,
        cost_estimate=pl.CostEstimate(flops=1 << 29, bytes_accessed=2 << 20, transcendentals=0),
    )(lanes, mine, theirs, resid, rows)


def moved(shard, where):
    sections, devices = lax.axis_size("section"), lax.axis_size("expert")
    route = []
    for s in range(sections):
        for i in range(devices):
            to_s, to_i = where(s, i)
            route.append((s * devices + i, to_s % sections * devices + to_i))
    return lax.ppermute(shard, ("section", "expert"), route)


def across_cores(shard):
    return moved(shard, lambda s, i: (s ^ 1, i))


def swapped(shard, apart):
    return lax.ppermute(shard, "expert", [(i, i ^ apart) for i in range(lax.axis_size("expert"))])


def shifted(shard, apart):
    size = lax.axis_size("expert")
    return lax.ppermute(shard, "expert", [(i, (i + apart) % size) for i in range(size)])


def gathered_proj(piece, index):
    block = piece
    for apart in (4, 2, 1):
        other = swapped(block, apart)
        upper = (index & apart) != 0
        low = jnp.where(upper, other, block)
        high = jnp.where(upper, block, other)
        rows = piece.shape[0]
        shape = (block.shape[0] // rows, 1, rows, piece.shape[1])
        block = jnp.concatenate([low.reshape(shape), high.reshape(shape)], axis=1)
        block = block.reshape(-1, piece.shape[1])
    onward, backward = [block], [block]
    for step in range(4):
        onward.append(shifted(onward[-1], SIDE))
        if step < 3:
            backward.append(shifted(backward[-1], -SIDE))
    return onward + backward[1:]


def exchanged(blocks, devices):
    rows, width = blocks.shape
    sent = blocks.reshape(devices, rows // devices, width)
    return lax.all_to_all(sent, "expert", split_axis=0, concat_axis=0, tiled=True).reshape(rows, width)


def shards(histories, page_map, user_pages, tails, routes, out_proj, router, w_gate, w_up, w_down):
    devices = lax.axis_size("expert")
    index = lax.axis_index("expert")
    count = histories.shape[1]
    experts = router.shape[2]
    weights = dict(gate=w_gate[0], up=w_up[0], down=w_down[0])
    mine = routes[0].T
    first = {}

    def trade(name):
        first[name] = moved(
            weights[name], lambda s, i: (s, i) if s % 2 == i % 2 else (s ^ 1, i ^ 1)
        )

    trade("gate")
    outgoing = pack_pages(page_map, histories[0], devices)
    arrived = exchanged(outgoing, devices)
    arrived, weights["up"], weights["down"] = lax.optimization_barrier(
        (arrived, weights["up"], weights["down"])
    )
    trade("up")
    trade("down")
    theirs = across_cores(mine)
    core = (lax.axis_index("section") & 1).astype(jnp.int32).reshape(1)
    pick, lanes = slot_tables(core, mine, theirs, experts)
    proj = gathered_proj(out_proj[0], index)
    place = lax.shift_right_logical(index, 3).astype(jnp.int32).reshape(1)
    normed, resid, share = token_stage(
        place, user_pages, tails, page_map, mine, arrived, router[0].T, proj, count
    )
    other_rows = across_cores(normed)
    other_share = across_cores(share)
    packed = pack_rows(pick, normed, other_rows)
    rows = exchanged(packed, devices)
    second = {}
    for name in weights:
        second[name] = across_cores(first[name])
    served = expert_half(rows, first["gate"], first["up"], first["down"])
    served = expert_half(rows, second["gate"], second["up"], second["down"], served)
    result = exchanged(served, devices)
    own, other = combine(lanes, share, other_share, resid, result)
    own = moved(own, lambda s, i: (s + 1, i))
    other = moved(other, lambda s, i: (s, i) if s % 2 else (s + 2, i))
    return (own.astype(F32) + other.astype(F32)).astype(BF16)[None]


def solution(mesh):
    in_specs = (
        P("section", "expert", None),
        P("section", None, "expert"),
        P("section", "expert", None),
        P("section", "expert", None),
        P("section", "expert", None),
        P("section", "expert", None),
        P("section", None, None),
        P("section", None, "expert"),
        P("section", None, "expert"),
        P("section", "expert", None),
    )
    out_specs = P("section", "expert", None)
    return jax.shard_map(
        shards, mesh=mesh, in_specs=in_specs, out_specs=out_specs, check_vma=False
    )
```

```python
import functools

import jax
import jax.numpy as jnp
from jax import lax
from jax.experimental import pallas as pl
from jax.experimental.pallas import tpu as pltpu
from jax.sharding import PartitionSpec as P


HEADS = 8
F32 = jnp.float32
BF16 = jnp.bfloat16
VMEM = pltpu.VMEM
SMEM = pltpu.SMEM


def iota(shape, axis):
    return lax.broadcasted_iota(jnp.int32, shape, axis)


def dot(a, b):
    return jnp.dot(a, b, preferred_element_type=F32)


def dot_t(a, b):
    return lax.dot_general(a, b, (((1,), (1,)), ((), ())), preferred_element_type=F32)


def flag(mask):
    return jnp.where(mask, 1.0, 0.0).astype(BF16)


def whole(space=VMEM):
    return pl.BlockSpec(memory_space=space)


def pack_pages_body(map_ref, rows_ref, out_ref, pick_ref):
    @pl.when(pl.program_id(0) == 0)
    def _():
        device = lax.shift_right_logical(map_ref[0, 0:1, :], 5).astype(F32)
        pages = device.shape[1]
        rows = pages * 4
        spread = flag(iota((pages, rows), 0) == lax.shift_right_logical(iota((pages, rows), 1), 2))
        target = dot(jnp.broadcast_to(device, (8, pages)).astype(BF16), spread)[0:1]
        slot = iota((pick_ref.shape[0], rows), 0)
        row = iota((pick_ref.shape[0], rows), 1)
        hit = (lax.shift_right_logical(slot, 3) == target.astype(jnp.int32)) & ((slot & 3) == (row & 3))
        pick_ref[:, :rows] = flag(hit & ((slot & 4) == 0))
        pick_ref[:, rows:] = flag(hit & ((slot & 4) == 4))

    half = rows_ref.shape[1] // 2
    both = jnp.concatenate([rows_ref[:, :half], rows_ref[:, half:]], axis=0)
    out_ref[...] = dot(pick_ref[...], both).astype(BF16)


def pack_pages(page_map, rows, devices):
    count, width = rows.shape
    block = width // 5
    slots = devices * 8
    return pl.pallas_call(
        pack_pages_body,
        name="pack_pages",
        grid=(5,),
        in_specs=[
            whole(),
            pl.BlockSpec((count, block), lambda b: (0, b)),
        ],
        out_specs=pl.BlockSpec((slots, block // 2), lambda b: (0, b)),
        out_shape=jax.ShapeDtypeStruct((slots, width // 2), BF16),
        scratch_shapes=[pltpu.VMEM((slots, 2 * count), BF16)],
        cost_estimate=pl.CostEstimate(flops=1 << 30, bytes_accessed=4 << 20, transcendentals=0),
    )(page_map, rows)


def user_layout(index, pages_ref, tails_ref):
    users = pages_ref.shape[2]
    owner = jnp.zeros_like(index)
    offset = jnp.zeros_like(index)
    length = jnp.zeros_like(index) + ((pages_ref[0, 0, 0] - 1) * 4 + tails_ref[0, 0, 0])
    start = 0
    for user in range(1, users):
        start = start + pages_ref[0, 0, user - 1] * 4
        inside = index >= start
        owner = jnp.where(inside, user, owner)
        offset = jnp.where(inside, start, offset)
        length = jnp.where(inside, (pages_ref[0, 0, user] - 1) * 4 + tails_ref[0, 0, user], length)
    return owner, offset, length


def token_body(
    pages_ref,
    tails_ref,
    map_ref,
    routes_ref,
    router_ref,
    arrived_hbm,
    proj_hbm,
    normed_ref,
    resid_ref,
    share_ref,
    arrived_ref,
    proj_ref,
    mixed_ref,
    sems,
):
    count, model_width = resid_ref.shape
    slots = arrived_ref.shape[0]
    half = arrived_ref.shape[1] // 5
    pages = map_ref.shape[2]
    head_dim = model_width // HEADS
    copies = []
    for index in range(5):
        part = pl.ds(index * half, half)
        copies.append(
            pltpu.make_async_copy(arrived_hbm.at[:, part], arrived_ref.at[:, part], sems.at[index])
        )
    copies.append(pltpu.make_async_copy(proj_hbm, proj_ref, sems.at[5]))
    for copy in copies:
        copy.start()

    source = lax.shift_right_logical(map_ref[0, 1:2, :], 5).astype(F32)
    mine = lax.shift_right_logical(iota((count, pages), 0), 2) == iota((count, pages), 1)
    source = jnp.sum(jnp.where(mine, source, 0.0), axis=1, keepdims=True).astype(jnp.int32)
    slot = iota((count, slots), 1)
    near = lax.shift_right_logical(slot, 3) == source
    row = iota((count, slots), 0) & 3
    picks = [flag(near & ((slot & 7) == row + 4 * side)) for side in range(2)]

    def block(index, side):
        if side == 0:
            copies[index].wait()
        return dot(picks[side], arrived_ref[:, index * half : (index + 1) * half])

    rows = iota((count, count), 0)
    keys = iota((count, count), 1)
    row_owner, _, row_length = user_layout(rows, pages_ref, tails_ref)
    key_owner, key_offset, key_length = user_layout(keys, pages_ref, tails_ref)
    allowed = (row_owner == key_owner) & (keys <= rows) & (keys - key_offset < key_length)
    factor = jnp.where(allowed, 1.0 / row_length.astype(F32), 0.0)
    attended = []
    blocks = [[block(index, side).astype(BF16) for side in range(2)] for index in range(3)]
    for side in range(2):
        queries, key_rows, values = [blocks[index][side] for index in range(3)]
        for head in range(HEADS // 2):
            part = slice(head * head_dim, (head + 1) * head_dim)
            scores = dot_t(queries[:, part], key_rows[:, part]) * head_dim ** (-0.5)
            weights = (scores * jax.nn.sigmoid(scores) * factor).astype(BF16)
            attended.append(dot(weights, values[:, part]))
    total = functools.reduce(jnp.add, attended)
    average = jnp.sum(total, axis=1, keepdims=True) * (1.0 / model_width)
    attended = [part - average for part in attended]
    squares = functools.reduce(jnp.add, [part * part for part in attended])
    variance = jnp.sum(squares, axis=1, keepdims=True) * (1.0 / model_width)
    scale = lax.rsqrt(variance + 1e-05)
    for side in range(2):
        gating = block(3, side)
        for head in range(HEADS // 2):
            part = slice(head * head_dim, (head + 1) * head_dim)
            index = side * (HEADS // 2) + head
            mixed = attended[index] * scale * gating[:, part]
            mixed_ref[:, index * head_dim : (index + 1) * head_dim] = mixed.astype(BF16)

    squares = jnp.zeros((count, 1), F32)
    chunk = half // 2
    for side in range(2):
        inputs = block(4, side)
        if side == 0:
            copies[5].wait()
        for quarter in range(2):
            part = slice(side * half + quarter * chunk, side * half + (quarter + 1) * chunk)
            projected = dot(mixed_ref[...], proj_ref[:, part])
            resid = (inputs[:, quarter * chunk : (quarter + 1) * chunk] + projected).astype(BF16)
            resid_ref[:, part] = resid
            wide = resid.astype(F32)
            squares += jnp.sum(wide * wide, axis=1, keepdims=True)
    scale = lax.rsqrt(squares * (1.0 / model_width) + 1e-06)
    for quarter in range(4):
        part = slice(quarter * chunk, (quarter + 1) * chunk)
        normed_ref[:, part] = (resid_ref[:, part].astype(F32) * scale).astype(BF16)

    experts = router_ref.shape[0]
    scores = jax.nn.sigmoid(dot_t(router_ref[...], normed_ref[...]))
    expert = iota((experts, count), 0)
    chosen = [
        jnp.sum(jnp.where(expert == routes_ref[k : k + 1, :], scores, 0.0), axis=0, keepdims=True)
        for k in range(2)
    ]
    share_ref[...] = jnp.zeros(share_ref.shape, F32)
    for k in range(2):
        share_ref[k : k + 1, :] = chosen[k] / (chosen[0] + chosen[1])


def token_stage(user_pages, tails, page_map, routes, router, arrived, proj, count):
    width = proj.shape[1]
    return pl.pallas_call(
        token_body,
        name="token_stage",
        in_specs=[whole(SMEM)] * 2 + [whole()] * 3 + [whole(pl.ANY)] * 2,
        out_specs=[whole()] * 3,
        out_shape=[
            jax.ShapeDtypeStruct((count, width), BF16),
            jax.ShapeDtypeStruct((count, width), BF16),
            jax.ShapeDtypeStruct((8, count), F32),
        ],
        scratch_shapes=[
            pltpu.VMEM(arrived.shape, BF16),
            pltpu.VMEM(proj.shape, BF16),
            pltpu.VMEM((count, width), BF16),
            pltpu.SemaphoreType.DMA((6,)),
        ],
        compiler_params=pltpu.CompilerParams(vmem_limit_bytes=40 << 20),
        cost_estimate=pl.CostEstimate(flops=2 << 30, bytes_accessed=6 << 20, transcendentals=0),
    )(user_pages, tails, page_map, routes, router, arrived, proj)


def slots_body(experts, core_ref, mine_ref, theirs_ref, pick_ref, lanes_ref):
    count = mine_ref.shape[1]
    core = core_ref[0]
    capacity = 4 * count // experts
    expert = iota((experts, count), 0)
    earlier = flag(iota((count, count), 0) < iota((count, count), 1))
    row = iota((pick_ref.shape[0], count), 0)
    lanes_ref[...] = jnp.zeros(lanes_ref.shape, F32)
    for side, routes_ref in enumerate((mine_ref, theirs_ref)):
        chosen = [routes_ref[k : k + 1, :] for k in range(2)]
        named = [expert == chosen[k] for k in range(2)]
        before = dot(flag(named[0] | named[1]), earlier)
        lanes = []
        for k in range(2):
            rank = jnp.sum(jnp.where(named[k], before, 0.0), axis=0, keepdims=True)
            slot = chosen[k] * capacity + rank.astype(jnp.int32)
            half = lax.shift_right_logical(slot, 3) & 1
            lanes.append(jnp.where(half == core, slot ^ (8 * side), -1))
            lanes_ref[2 * side + k : 2 * side + k + 1, :] = lanes[k].astype(F32)
        pick_ref[:, side * count : (side + 1) * count] = flag((row == lanes[0]) | (row == lanes[1]))


def slot_tables(core, mine, theirs, experts):
    count = mine.shape[1]
    rows = 4 * count
    return pl.pallas_call(
        functools.partial(slots_body, experts),
        name="slot_tables",
        in_specs=[whole(SMEM), whole(), whole()],
        out_specs=[whole()] * 2,
        out_shape=[
            jax.ShapeDtypeStruct((rows, 2 * count), BF16),
            jax.ShapeDtypeStruct((8, count), F32),
        ],
        compiler_params=pltpu.CompilerParams(vmem_limit_bytes=4 << 20),
        cost_estimate=pl.CostEstimate(flops=1 << 24, bytes_accessed=1 << 18, transcendentals=0),
    )(core, mine, theirs)


def pack_rows_body(pick_ref, mine_ref, theirs_hbm, out_ref, theirs_ref, sem):
    copy = pltpu.make_async_copy(theirs_hbm, theirs_ref, sem)
    copy.start()
    copy.wait()
    _, width = mine_ref.shape
    chunk = width // 4
    for quarter in range(4):
        part = slice(quarter * chunk, (quarter + 1) * chunk)
        rows = jnp.concatenate([mine_ref[:, part], theirs_ref[:, part]], axis=0)
        out_ref[:, part] = dot(pick_ref[...], rows).astype(BF16)


def pack_rows(pick, mine, theirs):
    return pl.pallas_call(
        pack_rows_body,
        name="pack_rows",
        in_specs=[whole(), whole(), whole(pl.ANY)],
        out_specs=whole(),
        out_shape=jax.ShapeDtypeStruct((pick.shape[0], mine.shape[1]), BF16),
        scratch_shapes=[pltpu.VMEM(theirs.shape, BF16), pltpu.SemaphoreType.DMA],
        compiler_params=pltpu.CompilerParams(vmem_limit_bytes=4 << 20),
        cost_estimate=pl.CostEstimate(flops=1 << 28, bytes_accessed=2 << 20, transcendentals=0),
    )(pick, mine, theirs)


def expert_body(
    rows_hbm,
    gate_hbm,
    up_hbm,
    down_hbm,
    out_ref,
    rows_ref,
    gate_ref,
    up_ref,
    down_ref,
    hidden_ref,
    sems,
):
    units = hidden_ref.shape[1]
    chunk = units // 2
    width = out_ref.shape[1]
    rows_copy = pltpu.make_async_copy(rows_hbm, rows_ref, sems.at[0])
    rows_copy.start()
    copies = []
    for half in range(2):
        for piece in range(2):
            part = pl.ds(piece * chunk, chunk)
            for hbm, ref in ((gate_hbm, gate_ref), (up_hbm, up_ref)):
                copies.append(
                    pltpu.make_async_copy(
                        hbm.at[half, :, part], ref.at[half, :, part], sems.at[1 + len(copies)]
                    )
                )
        copies.append(
            pltpu.make_async_copy(down_hbm.at[half], down_ref.at[half], sems.at[1 + len(copies)])
        )
    for copy in copies:
        copy.start()
    rows_copy.wait()
    pending = iter(copies)
    for half in range(2):
        for piece in range(2):
            part = slice(piece * chunk, (piece + 1) * chunk)
            next(pending).wait()
            gate = dot(rows_ref[...], gate_ref[half, :, part])
            next(pending).wait()
            hidden = gate * jax.nn.sigmoid(gate) * dot(rows_ref[...], up_ref[half, :, part])
            hidden_ref[:, part] = hidden.astype(BF16)
        next(pending).wait()
        for quarter in range(4):
            part = slice(quarter * width // 4, (quarter + 1) * width // 4)
            result = dot(hidden_ref[...], down_ref[half, :, part]).astype(BF16)
            if half == 1:
                result = (out_ref[:, part].astype(F32) + result.astype(F32)).astype(BF16)
            out_ref[:, part] = result


def expert_stage(rows, gate, up, down):
    count, width = rows.shape
    units = gate.shape[2]
    return pl.pallas_call(
        expert_body,
        name="expert_stage",
        in_specs=[whole(pl.ANY)] * 4,
        out_specs=whole(),
        out_shape=jax.ShapeDtypeStruct((count, width), BF16),
        scratch_shapes=[
            pltpu.VMEM((count, width), BF16),
            pltpu.VMEM(gate.shape, BF16),
            pltpu.VMEM(up.shape, BF16),
            pltpu.VMEM(down.shape, BF16),
            pltpu.VMEM((count, units), BF16),
            pltpu.SemaphoreType.DMA((11,)),
        ],
        compiler_params=pltpu.CompilerParams(vmem_limit_bytes=50 << 20),
        cost_estimate=pl.CostEstimate(flops=4 << 30, bytes_accessed=8 << 20, transcendentals=0),
    )(rows, gate, up, down)


def combine_body(
    lanes_ref, mine_ref, theirs_ref, resid_ref, rows_hbm, own_ref, other_ref, rows_ref, sem
):
    copy = pltpu.make_async_copy(rows_hbm, rows_ref, sem)
    copy.start()
    count, width = resid_ref.shape
    slots = rows_ref.shape[0]
    table = jnp.concatenate([lanes_ref[0:4, :], mine_ref[0:2, :], theirs_ref[0:2, :]], axis=0)
    table = jnp.transpose(table)
    slot = iota((count, slots), 1).astype(F32)
    shares = []
    for side in range(2):
        share = jnp.zeros((count, slots), F32)
        for k in range(2):
            lane = 2 * side + k
            share += jnp.where(slot == table[:, lane : lane + 1], table[:, 4 + lane : 5 + lane], 0.0)
        high = share.astype(BF16)
        shares.append((high, (share - high.astype(F32)).astype(BF16)))
    chunk = width // 4
    copy.wait()
    for quarter in range(4):
        part = slice(quarter * chunk, (quarter + 1) * chunk)
        rows = rows_ref[:, part]
        own, other = [dot(high, rows) + dot(low, rows) for high, low in shares]
        own_ref[:, part] = (resid_ref[:, part].astype(F32) + own).astype(BF16)
        other_ref[:, part] = other.astype(BF16)


def combine(lanes, mine, theirs, resid, rows):
    return pl.pallas_call(
        combine_body,
        name="combine",
        in_specs=[whole()] * 4 + [whole(pl.ANY)],
        out_specs=[whole()] * 2,
        out_shape=[jax.ShapeDtypeStruct(resid.shape, BF16)] * 2,
        scratch_shapes=[pltpu.VMEM(rows.shape, BF16), pltpu.SemaphoreType.DMA],
        compiler_params=pltpu.CompilerParams(vmem_limit_bytes=10 << 20),
        cost_estimate=pl.CostEstimate(flops=1 << 29, bytes_accessed=2 << 20, transcendentals=0),
    )(lanes, mine, theirs, resid, rows)


def moved(shard, where):
    sections, devices = lax.axis_size("section"), lax.axis_size("expert")
    route = []
    for s in range(sections):
        for i in range(devices):
            to_s, to_i = where(s, i)
            route.append((s * devices + i, to_s % sections * devices + to_i))
    return lax.ppermute(shard, ("section", "expert"), route)


def across_cores(shard):
    return moved(shard, lambda s, i: (s ^ 1, i))


def exchanged(blocks, devices):
    rows, width = blocks.shape
    sent = blocks.reshape(devices, rows // devices, width)
    return lax.all_to_all(sent, "expert", split_axis=0, concat_axis=0, tiled=True).reshape(rows, width)


def traded(weight):
    sections, devices = lax.axis_size("section"), lax.axis_size("expert")
    groups = []
    for s in range(sections):
        for i in range(devices):
            partner = ((s ^ 1), (i ^ 1)) if s % 2 != i % 2 else (s ^ 2 if sections > 2 else s, i ^ 2 * (sections == 2))
            me, other = s * devices + i, partner[0] * devices + partner[1]
            if me < other:
                groups.append([me, other])
    pair = lax.all_gather(weight, ("section", "expert"), axis_index_groups=groups)
    section, index = lax.axis_index("section"), lax.axis_index("expert")
    core = section & 1
    spot = (section >> 1) & 1 if sections > 2 else (index >> 1) & 1
    return lax.dynamic_index_in_dim(pair, jnp.where(core != (index & 1), 1 - core, spot), keepdims=False)


def shards(histories, page_map, user_pages, tails, routes, out_proj, router, w_gate, w_up, w_down):
    devices = lax.axis_size("expert")
    count = histories.shape[1]
    experts = router.shape[2]
    weights = dict(gate=w_gate[0], up=w_up[0], down=w_down[0])
    mine = routes[0].T
    pairs = [[s, s + 1] for s in range(0, lax.axis_size("section"), 2)]
    proj = lax.all_gather(out_proj[0], "expert", axis=0, tiled=True)
    theirs = across_cores(mine)
    outgoing = pack_pages(page_map, histories[0], devices)
    arrived = exchanged(outgoing, devices)
    both = {}
    for name, weight in weights.items():
        first = traded(weight)
        both[name] = lax.all_gather(first, "section", axis_index_groups=pairs)
    core = (lax.axis_index("section") & 1).astype(jnp.int32).reshape(1)
    pick, lanes = slot_tables(core, mine, theirs, experts)
    normed, resid, share = token_stage(
        user_pages, tails, page_map, mine, router[0].T, arrived, proj, count
    )
    other_rows = across_cores(normed)
    packed = pack_rows(pick, normed, other_rows)
    rows = exchanged(packed, devices)
    other_share = across_cores(share)
    served = expert_stage(rows, both["gate"], both["up"], both["down"])
    result = exchanged(served, devices)
    own, other = combine(lanes, share, other_share, resid, result)
    own = moved(own, lambda s, i: (s + 1, i))
    other = moved(other, lambda s, i: (s, i) if s % 2 else (s + 2, i))
    return (own.astype(F32) + other.astype(F32)).astype(BF16)[None]


def solution(mesh):
    in_specs = (
        P("section", "expert", None),
        P("section", None, "expert"),
        P("section", "expert", None),
        P("section", "expert", None),
        P("section", "expert", None),
        P("section", "expert", None),
        P("section", None, None),
        P("section", None, "expert"),
        P("section", None, "expert"),
        P("section", "expert", None),
    )
    out_specs = P("section", "expert", None)
    return jax.shard_map(
        shards, mesh=mesh, in_specs=in_specs, out_specs=out_specs, check_vma=False
    )
```

```python
import functools

import jax
import jax.numpy as jnp
from jax import lax
from jax.experimental import pallas as pl
from jax.experimental.pallas import tpu as pltpu
from jax.sharding import PartitionSpec as P


HEADS = 8
RING = (0, 1, 2, 3, 4, -1, -2, -3)
F32 = jnp.float32
BF16 = jnp.bfloat16
VMEM = pltpu.VMEM
SMEM = pltpu.SMEM


def iota(shape, axis):
    return lax.broadcasted_iota(jnp.int32, shape, axis)


def dot(a, b):
    return jnp.dot(a, b, preferred_element_type=F32)


def dot_t(a, b):
    return lax.dot_general(a, b, (((1,), (1,)), ((), ())), preferred_element_type=F32)


def flag(mask):
    return jnp.where(mask, 1.0, 0.0).astype(BF16)


def whole(space=VMEM):
    return pl.BlockSpec(memory_space=space)


def pack_pages_body(map_ref, rows_ref, out_ref, pick_ref):
    @pl.when(pl.program_id(0) == 0)
    def _():
        device = lax.shift_right_logical(map_ref[0, 0:1, :], 5).astype(F32)
        pages = device.shape[1]
        rows = pages * 4
        spread = flag(iota((pages, rows), 0) == lax.shift_right_logical(iota((pages, rows), 1), 2))
        target = dot(jnp.broadcast_to(device, (8, pages)).astype(BF16), spread)[0:1]
        slot = iota((pick_ref.shape[0], rows), 0)
        row = iota((pick_ref.shape[0], rows), 1)
        hit = (lax.shift_right_logical(slot, 3) == target.astype(jnp.int32)) & ((slot & 3) == (row & 3))
        pick_ref[:, :rows] = flag(hit & ((slot & 4) == 0))
        pick_ref[:, rows:] = flag(hit & ((slot & 4) == 4))

    half = rows_ref.shape[1] // 2
    both = jnp.concatenate([rows_ref[:, :half], rows_ref[:, half:]], axis=0)
    out_ref[...] = dot(pick_ref[...], both).astype(BF16)


def pack_pages(page_map, rows, devices):
    count, width = rows.shape
    block = width // 5
    slots = devices * 8
    return pl.pallas_call(
        pack_pages_body,
        name="pack_pages",
        grid=(5,),
        in_specs=[
            whole(),
            pl.BlockSpec((count, block), lambda b: (0, b)),
        ],
        out_specs=pl.BlockSpec((slots, block // 2), lambda b: (0, b)),
        out_shape=jax.ShapeDtypeStruct((slots, width // 2), BF16),
        scratch_shapes=[pltpu.VMEM((slots, 2 * count), BF16)],
        cost_estimate=pl.CostEstimate(flops=1 << 30, bytes_accessed=4 << 20, transcendentals=0),
    )(page_map, rows)


def user_layout(index, pages_ref, tails_ref):
    users = pages_ref.shape[2]
    owner = jnp.zeros_like(index)
    offset = jnp.zeros_like(index)
    length = jnp.zeros_like(index) + ((pages_ref[0, 0, 0] - 1) * 4 + tails_ref[0, 0, 0])
    start = 0
    for user in range(1, users):
        start = start + pages_ref[0, 0, user - 1] * 4
        inside = index >= start
        owner = jnp.where(inside, user, owner)
        offset = jnp.where(inside, start, offset)
        length = jnp.where(inside, (pages_ref[0, 0, user] - 1) * 4 + tails_ref[0, 0, user], length)
    return owner, offset, length


def token_body(
    pages_ref,
    tails_ref,
    map_ref,
    routes_ref,
    router_ref,
    place_ref,
    arrived_hbm,
    *refs,
):
    proj_hbm = refs[: len(RING)]
    normed_ref, resid_ref, share_ref, arrived_ref, proj_ref, mixed_ref, sems = refs[len(RING) :]
    count, model_width = resid_ref.shape
    slots = arrived_ref.shape[0]
    half = arrived_ref.shape[1] // 5
    pages = map_ref.shape[2]
    head_dim = model_width // HEADS
    copies = []
    for index in range(5):
        part = pl.ds(index * half, half)
        copies.append(
            pltpu.make_async_copy(arrived_hbm.at[:, part], arrived_ref.at[:, part], sems.at[index])
        )
    for index, shift in enumerate(RING):
        rows = proj_hbm[index].shape[0]
        start = pl.multiple_of(((place_ref[0] - shift) & (len(RING) - 1)) * rows, rows)
        target = proj_ref.at[pl.ds(start, rows)]
        copies.append(pltpu.make_async_copy(proj_hbm[index], target, sems.at[5 + index]))
    for copy in copies:
        copy.start()

    source = lax.shift_right_logical(map_ref[0, 1:2, :], 5).astype(F32)
    mine = lax.shift_right_logical(iota((count, pages), 0), 2) == iota((count, pages), 1)
    source = jnp.sum(jnp.where(mine, source, 0.0), axis=1, keepdims=True).astype(jnp.int32)
    slot = iota((count, slots), 1)
    near = lax.shift_right_logical(slot, 3) == source
    row = iota((count, slots), 0) & 3
    picks = [flag(near & ((slot & 7) == row + 4 * side)) for side in range(2)]

    def block(index, side):
        if side == 0:
            copies[index].wait()
        return dot(picks[side], arrived_ref[:, index * half : (index + 1) * half])

    rows = iota((count, count), 0)
    keys = iota((count, count), 1)
    row_owner, _, row_length = user_layout(rows, pages_ref, tails_ref)
    key_owner, key_offset, key_length = user_layout(keys, pages_ref, tails_ref)
    allowed = (row_owner == key_owner) & (keys <= rows) & (keys - key_offset < key_length)
    factor = jnp.where(allowed, 1.0 / row_length.astype(F32), 0.0)
    attended = []
    blocks = [[block(index, side).astype(BF16) for side in range(2)] for index in range(3)]
    for side in range(2):
        queries, key_rows, values = [blocks[index][side] for index in range(3)]
        for head in range(HEADS // 2):
            part = slice(head * head_dim, (head + 1) * head_dim)
            scores = dot_t(queries[:, part], key_rows[:, part]) * head_dim ** (-0.5)
            weights = (scores * jax.nn.sigmoid(scores) * factor).astype(BF16)
            attended.append(dot(weights, values[:, part]))
    total = functools.reduce(jnp.add, attended)
    average = jnp.sum(total, axis=1, keepdims=True) * (1.0 / model_width)
    attended = [part - average for part in attended]
    squares = functools.reduce(jnp.add, [part * part for part in attended])
    variance = jnp.sum(squares, axis=1, keepdims=True) * (1.0 / model_width)
    scale = lax.rsqrt(variance + 1e-05)
    for side in range(2):
        gating = block(3, side)
        for head in range(HEADS // 2):
            part = slice(head * head_dim, (head + 1) * head_dim)
            index = side * (HEADS // 2) + head
            mixed = attended[index] * scale * gating[:, part]
            mixed_ref[:, index * head_dim : (index + 1) * head_dim] = mixed.astype(BF16)

    squares = jnp.zeros((count, 1), F32)
    chunk = half // 2
    for side in range(2):
        inputs = block(4, side)
        if side == 0:
            for copy in copies[5:]:
                copy.wait()
        for quarter in range(2):
            part = slice(side * half + quarter * chunk, side * half + (quarter + 1) * chunk)
            projected = dot(mixed_ref[...], proj_ref[:, part])
            resid = (inputs[:, quarter * chunk : (quarter + 1) * chunk] + projected).astype(BF16)
            resid_ref[:, part] = resid
            wide = resid.astype(F32)
            squares += jnp.sum(wide * wide, axis=1, keepdims=True)
    scale = lax.rsqrt(squares * (1.0 / model_width) + 1e-06)
    for quarter in range(4):
        part = slice(quarter * chunk, (quarter + 1) * chunk)
        normed_ref[:, part] = (resid_ref[:, part].astype(F32) * scale).astype(BF16)

    experts = router_ref.shape[0]
    scores = jax.nn.sigmoid(dot_t(router_ref[...], normed_ref[...]))
    expert = iota((experts, count), 0)
    chosen = [
        jnp.sum(jnp.where(expert == routes_ref[k : k + 1, :], scores, 0.0), axis=0, keepdims=True)
        for k in range(2)
    ]
    share_ref[...] = jnp.zeros(share_ref.shape, F32)
    for k in range(2):
        share_ref[k : k + 1, :] = chosen[k] / (chosen[0] + chosen[1])


def token_stage(user_pages, tails, page_map, routes, router, place, arrived, proj, count):
    depth, width = proj[0].shape
    return pl.pallas_call(
        token_body,
        name="token_stage",
        in_specs=[whole(SMEM)] * 2 + [whole()] * 3 + [whole(SMEM)] + [whole(pl.ANY)] * (1 + len(RING)),
        out_specs=[whole()] * 3,
        out_shape=[
            jax.ShapeDtypeStruct((count, width), BF16),
            jax.ShapeDtypeStruct((count, width), BF16),
            jax.ShapeDtypeStruct((8, count), F32),
        ],
        scratch_shapes=[
            pltpu.VMEM(arrived.shape, BF16),
            pltpu.VMEM((depth * len(RING), width), BF16),
            pltpu.VMEM((count, width), BF16),
            pltpu.SemaphoreType.DMA((5 + len(RING),)),
        ],
        compiler_params=pltpu.CompilerParams(vmem_limit_bytes=40 << 20),
        cost_estimate=pl.CostEstimate(flops=2 << 30, bytes_accessed=6 << 20, transcendentals=0),
    )(user_pages, tails, page_map, routes, router, place, arrived, *proj)


def slots_body(experts, core_ref, mine_ref, theirs_ref, pick_ref, lanes_ref):
    count = mine_ref.shape[1]
    core = core_ref[0]
    capacity = 4 * count // experts
    expert = iota((experts, count), 0)
    earlier = flag(iota((count, count), 0) < iota((count, count), 1))
    row = iota((pick_ref.shape[0], count), 0)
    lanes_ref[...] = jnp.zeros(lanes_ref.shape, F32)
    for side, routes_ref in enumerate((mine_ref, theirs_ref)):
        chosen = [routes_ref[k : k + 1, :] for k in range(2)]
        named = [expert == chosen[k] for k in range(2)]
        before = dot(flag(named[0] | named[1]), earlier)
        lanes = []
        for k in range(2):
            rank = jnp.sum(jnp.where(named[k], before, 0.0), axis=0, keepdims=True)
            slot = chosen[k] * capacity + rank.astype(jnp.int32)
            half = lax.shift_right_logical(slot, 3) & 1
            lanes.append(jnp.where(half == core, slot ^ (8 * side), -1))
            lanes_ref[2 * side + k : 2 * side + k + 1, :] = lanes[k].astype(F32)
        pick_ref[:, side * count : (side + 1) * count] = flag((row == lanes[0]) | (row == lanes[1]))


def slot_tables(core, mine, theirs, experts):
    count = mine.shape[1]
    rows = 4 * count
    return pl.pallas_call(
        functools.partial(slots_body, experts),
        name="slot_tables",
        in_specs=[whole(SMEM), whole(), whole()],
        out_specs=[whole()] * 2,
        out_shape=[
            jax.ShapeDtypeStruct((rows, 2 * count), BF16),
            jax.ShapeDtypeStruct((8, count), F32),
        ],
        compiler_params=pltpu.CompilerParams(vmem_limit_bytes=4 << 20),
        cost_estimate=pl.CostEstimate(flops=1 << 24, bytes_accessed=1 << 18, transcendentals=0),
    )(core, mine, theirs)


def pack_rows_body(pick_ref, mine_ref, theirs_hbm, out_ref, theirs_ref, sem):
    copy = pltpu.make_async_copy(theirs_hbm, theirs_ref, sem)
    copy.start()
    copy.wait()
    _, width = mine_ref.shape
    chunk = width // 4
    for quarter in range(4):
        part = slice(quarter * chunk, (quarter + 1) * chunk)
        rows = jnp.concatenate([mine_ref[:, part], theirs_ref[:, part]], axis=0)
        out_ref[:, part] = dot(pick_ref[...], rows).astype(BF16)


def pack_rows(pick, mine, theirs):
    return pl.pallas_call(
        pack_rows_body,
        name="pack_rows",
        in_specs=[whole(), whole(), whole(pl.ANY)],
        out_specs=whole(),
        out_shape=jax.ShapeDtypeStruct((pick.shape[0], mine.shape[1]), BF16),
        scratch_shapes=[pltpu.VMEM(theirs.shape, BF16), pltpu.SemaphoreType.DMA],
        compiler_params=pltpu.CompilerParams(vmem_limit_bytes=4 << 20),
        cost_estimate=pl.CostEstimate(flops=1 << 28, bytes_accessed=2 << 20, transcendentals=0),
    )(pick, mine, theirs)


def expert_body(rows_hbm, *refs):
    weights_hbm = (refs[0:3], refs[3:6])
    out_ref, rows_ref, gate_ref, up_ref, down_ref, hidden_ref, sems = refs[6:]
    units = hidden_ref.shape[1]
    chunk = units // 2
    width = out_ref.shape[1]
    rows_copy = pltpu.make_async_copy(rows_hbm, rows_ref, sems.at[0])
    rows_copy.start()
    copies = []
    for half in range(2):
        gate_hbm, up_hbm, down_hbm = weights_hbm[half]
        for piece in range(2):
            part = pl.ds(piece * chunk, chunk)
            for hbm, ref in ((gate_hbm, gate_ref), (up_hbm, up_ref)):
                sem = sems.at[1 + len(copies)]
                copies.append(pltpu.make_async_copy(hbm.at[:, part], ref.at[half, :, part], sem))
        sem = sems.at[1 + len(copies)]
        copies.append(pltpu.make_async_copy(down_hbm, down_ref.at[half], sem))
    for copy in copies:
        copy.start()
    rows_copy.wait()
    pending = iter(copies)
    for half in range(2):
        for piece in range(2):
            part = slice(piece * chunk, (piece + 1) * chunk)
            next(pending).wait()
            gate = dot(rows_ref[...], gate_ref[half, :, part])
            next(pending).wait()
            hidden = gate * jax.nn.sigmoid(gate) * dot(rows_ref[...], up_ref[half, :, part])
            hidden_ref[:, part] = hidden.astype(BF16)
        next(pending).wait()
        for quarter in range(4):
            part = slice(quarter * width // 4, (quarter + 1) * width // 4)
            result = dot(hidden_ref[...], down_ref[half, :, part]).astype(BF16)
            if half == 1:
                result = (out_ref[:, part].astype(F32) + result.astype(F32)).astype(BF16)
            out_ref[:, part] = result


def expert_stage(rows, first, second):
    count, width = rows.shape
    units = first[0].shape[1]
    return pl.pallas_call(
        expert_body,
        name="expert_stage",
        in_specs=[whole(pl.ANY)] * 7,
        out_specs=whole(),
        out_shape=jax.ShapeDtypeStruct((count, width), BF16),
        scratch_shapes=[
            pltpu.VMEM((count, width), BF16),
            pltpu.VMEM((2, width, units), BF16),
            pltpu.VMEM((2, width, units), BF16),
            pltpu.VMEM((2, units, width), BF16),
            pltpu.VMEM((count, units), BF16),
            pltpu.SemaphoreType.DMA((11,)),
        ],
        compiler_params=pltpu.CompilerParams(vmem_limit_bytes=50 << 20),
        cost_estimate=pl.CostEstimate(flops=4 << 30, bytes_accessed=8 << 20, transcendentals=0),
    )(rows, *first, *second)


def combine_body(
    lanes_ref, mine_ref, theirs_ref, resid_ref, rows_hbm, own_ref, other_ref, rows_ref, sem
):
    copy = pltpu.make_async_copy(rows_hbm, rows_ref, sem)
    copy.start()
    count, width = resid_ref.shape
    slots = rows_ref.shape[0]
    table = jnp.concatenate([lanes_ref[0:4, :], mine_ref[0:2, :], theirs_ref[0:2, :]], axis=0)
    table = jnp.transpose(table)
    slot = iota((count, slots), 1).astype(F32)
    shares = []
    for side in range(2):
        share = jnp.zeros((count, slots), F32)
        for k in range(2):
            lane = 2 * side + k
            share += jnp.where(slot == table[:, lane : lane + 1], table[:, 4 + lane : 5 + lane], 0.0)
        high = share.astype(BF16)
        shares.append((high, (share - high.astype(F32)).astype(BF16)))
    chunk = width // 4
    copy.wait()
    for quarter in range(4):
        part = slice(quarter * chunk, (quarter + 1) * chunk)
        rows = rows_ref[:, part]
        own, other = [dot(high, rows) + dot(low, rows) for high, low in shares]
        own_ref[:, part] = (resid_ref[:, part].astype(F32) + own).astype(BF16)
        other_ref[:, part] = other.astype(BF16)


def combine(lanes, mine, theirs, resid, rows):
    return pl.pallas_call(
        combine_body,
        name="combine",
        in_specs=[whole()] * 4 + [whole(pl.ANY)],
        out_specs=[whole()] * 2,
        out_shape=[jax.ShapeDtypeStruct(resid.shape, BF16)] * 2,
        scratch_shapes=[pltpu.VMEM(rows.shape, BF16), pltpu.SemaphoreType.DMA],
        compiler_params=pltpu.CompilerParams(vmem_limit_bytes=10 << 20),
        cost_estimate=pl.CostEstimate(flops=1 << 29, bytes_accessed=2 << 20, transcendentals=0),
    )(lanes, mine, theirs, resid, rows)


def moved(shard, where):
    sections, devices = lax.axis_size("section"), lax.axis_size("expert")
    route = []
    for s in range(sections):
        for i in range(devices):
            to_s, to_i = where(s, i)
            route.append((s * devices + i, to_s % sections * devices + to_i))
    return lax.ppermute(shard, ("section", "expert"), route)


def across_cores(shard):
    return moved(shard, lambda s, i: (s ^ 1, i))


def exchanged(blocks, devices):
    rows, width = blocks.shape
    sent = blocks.reshape(devices, rows // devices, width)
    return lax.all_to_all(sent, "expert", split_axis=0, concat_axis=0, tiled=True).reshape(rows, width)


def shifted(shard, apart):
    size = lax.axis_size("expert")
    return lax.ppermute(shard, "expert", [(i, (i + apart) % size) for i in range(size)])


def gathered_proj(piece):
    side = len(RING)
    devices = lax.axis_size("expert")
    groups = [list(range(start, start + side)) for start in range(0, devices, side)]
    copies = jnp.broadcast_to(piece[None], (side,) + piece.shape)
    block = lax.all_to_all(
        copies, "expert", split_axis=0, concat_axis=0, tiled=True, axis_index_groups=groups
    )
    block = block.reshape(-1, piece.shape[1])
    blocks = {0: block}
    for step in range(1, side // 2 + 1):
        blocks[step] = shifted(blocks[step - 1], side)
        if step < side // 2:
            blocks[-step] = shifted(blocks[1 - step], -side)
    return [blocks[shift] for shift in RING]


def shards(histories, page_map, user_pages, tails, routes, out_proj, router, w_gate, w_up, w_down):
    devices = lax.axis_size("expert")
    count = histories.shape[1]
    experts = router.shape[2]
    weights = dict(gate=w_gate[0], up=w_up[0], down=w_down[0])
    mine = routes[0].T
    proj = gathered_proj(out_proj[0])
    first, second = [], []
    for weight in weights.values():
        first.append(moved(weight, lambda s, i: (s, i) if s % 2 == i % 2 else (s ^ 1, i ^ 1)))
        second.append(across_cores(first[-1]))
    outgoing = pack_pages(page_map, histories[0], devices)
    arrived = exchanged(outgoing, devices)
    theirs = across_cores(mine)
    core = (lax.axis_index("section") & 1).astype(jnp.int32).reshape(1)
    place = lax.shift_right_logical(lax.axis_index("expert"), 3).astype(jnp.int32).reshape(1)
    pick, lanes = slot_tables(core, mine, theirs, experts)
    normed, resid, share = token_stage(
        user_pages, tails, page_map, mine, router[0].T, place, arrived, proj, count
    )
    other_rows = across_cores(normed)
    packed = pack_rows(pick, normed, other_rows)
    rows = exchanged(packed, devices)
    other_share = across_cores(share)
    served = expert_stage(rows, first, second)
    result = exchanged(served, devices)
    own, other = combine(lanes, share, other_share, resid, result)
    own = moved(own, lambda s, i: (s + 1, i))
    other = moved(other, lambda s, i: (s, i) if s % 2 else (s + 2, i))
    return (own.astype(F32) + other.astype(F32)).astype(BF16)[None]


def solution(mesh):
    in_specs = (
        P("section", "expert", None),
        P("section", None, "expert"),
        P("section", "expert", None),
        P("section", "expert", None),
        P("section", "expert", None),
        P("section", "expert", None),
        P("section", None, None),
        P("section", None, "expert"),
        P("section", None, "expert"),
        P("section", "expert", None),
    )
    out_specs = P("section", "expert", None)
    return jax.shard_map(
        shards, mesh=mesh, in_specs=in_specs, out_specs=out_specs, check_vma=False
    )
```

```python
import functools

import jax
import jax.numpy as jnp
from jax import lax
from jax.experimental import pallas as pl
from jax.experimental.pallas import tpu as pltpu
from jax.sharding import PartitionSpec as P


HEADS = 8
RING = (0, 1, 2, 3, 4, -1, -2, -3)
F32 = jnp.float32
BF16 = jnp.bfloat16
VMEM = pltpu.VMEM
SMEM = pltpu.SMEM


def iota(shape, axis):
    return lax.broadcasted_iota(jnp.int32, shape, axis)


def dot(a, b):
    return jnp.dot(a, b, preferred_element_type=F32)


def dot_t(a, b):
    return lax.dot_general(a, b, (((1,), (1,)), ((), ())), preferred_element_type=F32)


def flag(mask):
    return jnp.where(mask, 1.0, 0.0).astype(BF16)


def whole(space=VMEM):
    return pl.BlockSpec(memory_space=space)


def pack_pages_body(map_ref, rows_ref, out_ref, pick_ref):
    @pl.when(pl.program_id(0) == 0)
    def _():
        device = lax.shift_right_logical(map_ref[0, 0:1, :], 5).astype(F32)
        pages = device.shape[1]
        rows = pages * 4
        spread = flag(iota((pages, rows), 0) == lax.shift_right_logical(iota((pages, rows), 1), 2))
        target = dot(jnp.broadcast_to(device, (8, pages)).astype(BF16), spread)[0:1]
        slot = iota((pick_ref.shape[0], rows), 0)
        row = iota((pick_ref.shape[0], rows), 1)
        hit = (lax.shift_right_logical(slot, 3) == target.astype(jnp.int32)) & ((slot & 3) == (row & 3))
        pick_ref[:, :rows] = flag(hit & ((slot & 4) == 0))
        pick_ref[:, rows:] = flag(hit & ((slot & 4) == 4))

    half = rows_ref.shape[1] // 2
    both = jnp.concatenate([rows_ref[:, :half], rows_ref[:, half:]], axis=0)
    out_ref[...] = dot(pick_ref[...], both).astype(BF16)


def pack_pages(page_map, rows, devices):
    count, width = rows.shape
    block = width // 5
    slots = devices * 8
    return pl.pallas_call(
        pack_pages_body,
        name="pack_pages",
        grid=(5,),
        in_specs=[
            whole(),
            pl.BlockSpec((count, block), lambda b: (0, b)),
        ],
        out_specs=pl.BlockSpec((slots, block // 2), lambda b: (0, b)),
        out_shape=jax.ShapeDtypeStruct((slots, width // 2), BF16),
        scratch_shapes=[pltpu.VMEM((slots, 2 * count), BF16)],
        cost_estimate=pl.CostEstimate(flops=1 << 30, bytes_accessed=4 << 20, transcendentals=0),
    )(page_map, rows)


def user_layout(index, pages_ref, tails_ref):
    users = pages_ref.shape[2]
    owner = jnp.zeros_like(index)
    offset = jnp.zeros_like(index)
    length = jnp.zeros_like(index) + ((pages_ref[0, 0, 0] - 1) * 4 + tails_ref[0, 0, 0])
    start = 0
    for user in range(1, users):
        start = start + pages_ref[0, 0, user - 1] * 4
        inside = index >= start
        owner = jnp.where(inside, user, owner)
        offset = jnp.where(inside, start, offset)
        length = jnp.where(inside, (pages_ref[0, 0, user] - 1) * 4 + tails_ref[0, 0, user], length)
    return owner, offset, length


def token_body(
    pages_ref,
    tails_ref,
    map_ref,
    routes_ref,
    router_ref,
    place_ref,
    arrived_hbm,
    *refs,
):
    proj_hbm = refs[: len(RING)]
    normed_ref, resid_ref, share_ref, arrived_ref, proj_ref, mixed_ref, sems = refs[len(RING) :]
    count, model_width = resid_ref.shape
    slots = arrived_ref.shape[0]
    half = arrived_ref.shape[1] // 5
    pages = map_ref.shape[2]
    head_dim = model_width // HEADS
    copies = []
    for index in range(5):
        part = pl.ds(index * half, half)
        copies.append(
            pltpu.make_async_copy(arrived_hbm.at[:, part], arrived_ref.at[:, part], sems.at[index])
        )
    for index, shift in enumerate(RING):
        rows = proj_hbm[index].shape[0]
        start = pl.multiple_of(((place_ref[0] - shift) & (len(RING) - 1)) * rows, rows)
        target = proj_ref.at[pl.ds(start, rows)]
        copies.append(pltpu.make_async_copy(proj_hbm[index], target, sems.at[5 + index]))
    for copy in copies:
        copy.start()

    source = lax.shift_right_logical(map_ref[0, 1:2, :], 5).astype(F32)
    mine = lax.shift_right_logical(iota((count, pages), 0), 2) == iota((count, pages), 1)
    source = jnp.sum(jnp.where(mine, source, 0.0), axis=1, keepdims=True).astype(jnp.int32)
    slot = iota((count, slots), 1)
    near = lax.shift_right_logical(slot, 3) == source
    row = iota((count, slots), 0) & 3
    picks = [flag(near & ((slot & 7) == row + 4 * side)) for side in range(2)]

    def block(index, side):
        if side == 0:
            copies[index].wait()
        return dot(picks[side], arrived_ref[:, index * half : (index + 1) * half])

    rows = iota((count, count), 0)
    keys = iota((count, count), 1)
    row_owner, _, row_length = user_layout(rows, pages_ref, tails_ref)
    key_owner, key_offset, key_length = user_layout(keys, pages_ref, tails_ref)
    allowed = (row_owner == key_owner) & (keys <= rows) & (keys - key_offset < key_length)
    factor = jnp.where(allowed, 1.0 / row_length.astype(F32), 0.0)
    attended = []
    blocks = [[block(index, side).astype(BF16) for side in range(2)] for index in range(3)]
    for side in range(2):
        queries, key_rows, values = [blocks[index][side] for index in range(3)]
        for head in range(HEADS // 2):
            part = slice(head * head_dim, (head + 1) * head_dim)
            scores = dot_t(queries[:, part], key_rows[:, part]) * head_dim ** (-0.5)
            weights = (scores * jax.nn.sigmoid(scores) * factor).astype(BF16)
            attended.append(dot(weights, values[:, part]))
    total = functools.reduce(jnp.add, attended)
    average = jnp.sum(total, axis=1, keepdims=True) * (1.0 / model_width)
    attended = [part - average for part in attended]
    squares = functools.reduce(jnp.add, [part * part for part in attended])
    variance = jnp.sum(squares, axis=1, keepdims=True) * (1.0 / model_width)
    scale = lax.rsqrt(variance + 1e-05)
    for side in range(2):
        gating = block(3, side)
        for head in range(HEADS // 2):
            part = slice(head * head_dim, (head + 1) * head_dim)
            index = side * (HEADS // 2) + head
            mixed = attended[index] * scale * gating[:, part]
            mixed_ref[:, index * head_dim : (index + 1) * head_dim] = mixed.astype(BF16)

    squares = jnp.zeros((count, 1), F32)
    chunk = half // 2
    for side in range(2):
        inputs = block(4, side)
        if side == 0:
            for copy in copies[5:]:
                copy.wait()
        for quarter in range(2):
            part = slice(side * half + quarter * chunk, side * half + (quarter + 1) * chunk)
            projected = dot(mixed_ref[...], proj_ref[:, part])
            resid = (inputs[:, quarter * chunk : (quarter + 1) * chunk] + projected).astype(BF16)
            resid_ref[:, part] = resid
            wide = resid.astype(F32)
            squares += jnp.sum(wide * wide, axis=1, keepdims=True)
    scale = lax.rsqrt(squares * (1.0 / model_width) + 1e-06)
    for quarter in range(4):
        part = slice(quarter * chunk, (quarter + 1) * chunk)
        normed_ref[:, part] = (resid_ref[:, part].astype(F32) * scale).astype(BF16)

    experts = router_ref.shape[0]
    scores = jax.nn.sigmoid(dot_t(router_ref[...], normed_ref[...]))
    expert = iota((experts, count), 0)
    chosen = [
        jnp.sum(jnp.where(expert == routes_ref[k : k + 1, :], scores, 0.0), axis=0, keepdims=True)
        for k in range(2)
    ]
    share_ref[...] = jnp.zeros(share_ref.shape, F32)
    for k in range(2):
        share_ref[k : k + 1, :] = chosen[k] / (chosen[0] + chosen[1])


def token_stage(user_pages, tails, page_map, routes, router, place, arrived, proj, count):
    depth, width = proj[0].shape
    return pl.pallas_call(
        token_body,
        name="token_stage",
        in_specs=[whole(SMEM)] * 2 + [whole()] * 3 + [whole(SMEM)] + [whole(pl.ANY)] * (1 + len(RING)),
        out_specs=[whole()] * 3,
        out_shape=[
            jax.ShapeDtypeStruct((count, width), BF16),
            jax.ShapeDtypeStruct((count, width), BF16),
            jax.ShapeDtypeStruct((8, count), F32),
        ],
        scratch_shapes=[
            pltpu.VMEM(arrived.shape, BF16),
            pltpu.VMEM((depth * len(RING), width), BF16),
            pltpu.VMEM((count, width), BF16),
            pltpu.SemaphoreType.DMA((5 + len(RING),)),
        ],
        compiler_params=pltpu.CompilerParams(vmem_limit_bytes=40 << 20),
        cost_estimate=pl.CostEstimate(flops=2 << 30, bytes_accessed=6 << 20, transcendentals=0),
    )(user_pages, tails, page_map, routes, router, place, arrived, *proj)


def slots_body(experts, core_ref, mine_ref, theirs_ref, pick_ref, lanes_ref):
    count = mine_ref.shape[1]
    core = core_ref[0]
    capacity = 4 * count // experts
    expert = iota((experts, count), 0)
    earlier = flag(iota((count, count), 0) < iota((count, count), 1))
    row = iota((pick_ref.shape[0], count), 0)
    lanes_ref[...] = jnp.zeros(lanes_ref.shape, F32)
    for side, routes_ref in enumerate((mine_ref, theirs_ref)):
        chosen = [routes_ref[k : k + 1, :] for k in range(2)]
        named = [expert == chosen[k] for k in range(2)]
        before = dot(flag(named[0] | named[1]), earlier)
        lanes = []
        for k in range(2):
            rank = jnp.sum(jnp.where(named[k], before, 0.0), axis=0, keepdims=True)
            slot = chosen[k] * capacity + rank.astype(jnp.int32)
            half = lax.shift_right_logical(slot, 3) & 1
            lanes.append(jnp.where(half == core, slot ^ (8 * side), -1))
            lanes_ref[2 * side + k : 2 * side + k + 1, :] = lanes[k].astype(F32)
        pick_ref[:, side * count : (side + 1) * count] = flag((row == lanes[0]) | (row == lanes[1]))


def slot_tables(core, mine, theirs, experts):
    count = mine.shape[1]
    rows = 4 * count
    return pl.pallas_call(
        functools.partial(slots_body, experts),
        name="slot_tables",
        in_specs=[whole(SMEM), whole(), whole()],
        out_specs=[whole()] * 2,
        out_shape=[
            jax.ShapeDtypeStruct((rows, 2 * count), BF16),
            jax.ShapeDtypeStruct((8, count), F32),
        ],
        compiler_params=pltpu.CompilerParams(vmem_limit_bytes=4 << 20),
        cost_estimate=pl.CostEstimate(flops=1 << 24, bytes_accessed=1 << 18, transcendentals=0),
    )(core, mine, theirs)


def pack_rows_body(pick_ref, mine_ref, theirs_hbm, out_ref, theirs_ref, sem):
    copy = pltpu.make_async_copy(theirs_hbm, theirs_ref, sem)
    copy.start()
    copy.wait()
    _, width = mine_ref.shape
    chunk = width // 4
    for quarter in range(4):
        part = slice(quarter * chunk, (quarter + 1) * chunk)
        rows = jnp.concatenate([mine_ref[:, part], theirs_ref[:, part]], axis=0)
        out_ref[:, part] = dot(pick_ref[...], rows).astype(BF16)


def pack_rows(pick, mine, theirs):
    return pl.pallas_call(
        pack_rows_body,
        name="pack_rows",
        in_specs=[whole(), whole(), whole(pl.ANY)],
        out_specs=whole(),
        out_shape=jax.ShapeDtypeStruct((pick.shape[0], mine.shape[1]), BF16),
        scratch_shapes=[pltpu.VMEM(theirs.shape, BF16), pltpu.SemaphoreType.DMA],
        compiler_params=pltpu.CompilerParams(vmem_limit_bytes=4 << 20),
        cost_estimate=pl.CostEstimate(flops=1 << 28, bytes_accessed=2 << 20, transcendentals=0),
    )(pick, mine, theirs)


def expert_body(rows_hbm, *refs):
    weights_hbm = (refs[0:3], refs[3:6])
    out_ref, rows_ref, gate_ref, up_ref, down_ref, hidden_ref, sems = refs[6:]
    units = hidden_ref.shape[1]
    chunk = units // 2
    width = out_ref.shape[1]
    rows_copy = pltpu.make_async_copy(rows_hbm, rows_ref, sems.at[0])
    rows_copy.start()
    copies = []
    for half in range(2):
        gate_hbm, up_hbm, down_hbm = weights_hbm[half]
        for piece in range(2):
            part = pl.ds(piece * chunk, chunk)
            for hbm, ref in ((gate_hbm, gate_ref), (up_hbm, up_ref)):
                sem = sems.at[1 + len(copies)]
                copies.append(pltpu.make_async_copy(hbm.at[:, part], ref.at[half, :, part], sem))
        sem = sems.at[1 + len(copies)]
        copies.append(pltpu.make_async_copy(down_hbm, down_ref.at[half], sem))
    for copy in copies:
        copy.start()
    rows_copy.wait()
    pending = iter(copies)
    for half in range(2):
        for piece in range(2):
            part = slice(piece * chunk, (piece + 1) * chunk)
            next(pending).wait()
            gate = dot(rows_ref[...], gate_ref[half, :, part])
            next(pending).wait()
            hidden = gate * jax.nn.sigmoid(gate) * dot(rows_ref[...], up_ref[half, :, part])
            hidden_ref[:, part] = hidden.astype(BF16)
        next(pending).wait()
        for quarter in range(4):
            part = slice(quarter * width // 4, (quarter + 1) * width // 4)
            result = dot(hidden_ref[...], down_ref[half, :, part]).astype(BF16)
            if half == 1:
                result = (out_ref[:, part].astype(F32) + result.astype(F32)).astype(BF16)
            out_ref[:, part] = result


def expert_stage(rows, first, second):
    count, width = rows.shape
    units = first[0].shape[1]
    return pl.pallas_call(
        expert_body,
        name="expert_stage",
        in_specs=[whole(pl.ANY)] * 7,
        out_specs=whole(),
        out_shape=jax.ShapeDtypeStruct((count, width), BF16),
        scratch_shapes=[
            pltpu.VMEM((count, width), BF16),
            pltpu.VMEM((2, width, units), BF16),
            pltpu.VMEM((2, width, units), BF16),
            pltpu.VMEM((2, units, width), BF16),
            pltpu.VMEM((count, units), BF16),
            pltpu.SemaphoreType.DMA((11,)),
        ],
        compiler_params=pltpu.CompilerParams(vmem_limit_bytes=50 << 20),
        cost_estimate=pl.CostEstimate(flops=4 << 30, bytes_accessed=8 << 20, transcendentals=0),
    )(rows, *first, *second)


def combine_body(
    lanes_ref, mine_ref, theirs_ref, resid_ref, rows_hbm, own_ref, other_ref, rows_ref, sem
):
    copy = pltpu.make_async_copy(rows_hbm, rows_ref, sem)
    copy.start()
    count, width = resid_ref.shape
    slots = rows_ref.shape[0]
    table = jnp.concatenate([lanes_ref[0:4, :], mine_ref[0:2, :], theirs_ref[0:2, :]], axis=0)
    table = jnp.transpose(table)
    slot = iota((count, slots), 1).astype(F32)
    shares = []
    for side in range(2):
        share = jnp.zeros((count, slots), F32)
        for k in range(2):
            lane = 2 * side + k
            share += jnp.where(slot == table[:, lane : lane + 1], table[:, 4 + lane : 5 + lane], 0.0)
        high = share.astype(BF16)
        shares.append((high, (share - high.astype(F32)).astype(BF16)))
    chunk = width // 4
    copy.wait()
    for quarter in range(4):
        part = slice(quarter * chunk, (quarter + 1) * chunk)
        rows = rows_ref[:, part]
        own, other = [dot(high, rows) + dot(low, rows) for high, low in shares]
        own_ref[:, part] = (resid_ref[:, part].astype(F32) + own).astype(BF16)
        other_ref[:, part] = other.astype(BF16)


def combine(lanes, mine, theirs, resid, rows):
    return pl.pallas_call(
        combine_body,
        name="combine",
        in_specs=[whole()] * 4 + [whole(pl.ANY)],
        out_specs=[whole()] * 2,
        out_shape=[jax.ShapeDtypeStruct(resid.shape, BF16)] * 2,
        scratch_shapes=[pltpu.VMEM(rows.shape, BF16), pltpu.SemaphoreType.DMA],
        compiler_params=pltpu.CompilerParams(vmem_limit_bytes=10 << 20),
        cost_estimate=pl.CostEstimate(flops=1 << 29, bytes_accessed=2 << 20, transcendentals=0),
    )(lanes, mine, theirs, resid, rows)


def moved(shard, where):
    sections, devices = lax.axis_size("section"), lax.axis_size("expert")
    route = []
    for s in range(sections):
        for i in range(devices):
            to_s, to_i = where(s, i)
            if (to_s, to_i) != (s, i):
                route.append((s * devices + i, to_s % sections * devices + to_i))
    return lax.ppermute(shard, ("section", "expert"), route)


def across_cores(shard):
    return moved(shard, lambda s, i: (s ^ 1, i))


def exchanged(blocks, devices):
    rows, width = blocks.shape
    sent = blocks.reshape(devices, rows // devices, width)
    return lax.all_to_all(sent, "expert", split_axis=0, concat_axis=0, tiled=True).reshape(rows, width)


def shifted(shard, apart):
    size = lax.axis_size("expert")
    return lax.ppermute(shard, "expert", [(i, (i + apart) % size) for i in range(size)])


def column_block(piece):
    side = len(RING)
    devices = lax.axis_size("expert")
    groups = [list(range(start, start + side)) for start in range(0, devices, side)]
    copies = jnp.broadcast_to(piece[None], (side,) + piece.shape)
    block = lax.all_to_all(
        copies, "expert", split_axis=0, concat_axis=0, tiled=True, axis_index_groups=groups
    )
    return block.reshape(-1, piece.shape[1])


def ringed(block):
    side = len(RING)
    blocks = {0: block}
    for step in range(1, side // 2 + 1):
        blocks[step] = shifted(blocks[step - 1], side)
        if step < side // 2:
            blocks[-step] = shifted(blocks[1 - step], -side)
    return [blocks[shift] for shift in RING]


def shards(histories, page_map, user_pages, tails, routes, out_proj, router, w_gate, w_up, w_down):
    devices = lax.axis_size("expert")
    count = histories.shape[1]
    experts = router.shape[2]
    weights = dict(gate=w_gate[0], up=w_up[0], down=w_down[0])
    mine = routes[0].T
    block = column_block(out_proj[0])
    weights = dict(zip(weights, lax.optimization_barrier((*weights.values(), block))))
    first, second = [], []
    odd = (lax.axis_index("section") & 1) == 1
    trader = odd != ((lax.axis_index("expert") & 1) == 1)
    for weight in weights.values():
        got = moved(weight, lambda s, i: (s, i) if s % 2 == i % 2 else (s ^ 1, i ^ 1))
        first.append(jnp.where(trader, got, weight))
        second.append(across_cores(first[-1]))
    proj = ringed(block)
    outgoing = pack_pages(page_map, histories[0], devices)
    arrived = exchanged(outgoing, devices)
    theirs = across_cores(mine)
    core = (lax.axis_index("section") & 1).astype(jnp.int32).reshape(1)
    place = lax.shift_right_logical(lax.axis_index("expert"), 3).astype(jnp.int32).reshape(1)
    pick, lanes = slot_tables(core, mine, theirs, experts)
    normed, resid, share = token_stage(
        user_pages, tails, page_map, mine, router[0].T, place, arrived, proj, count
    )
    other_rows = across_cores(normed)
    packed = pack_rows(pick, normed, other_rows)
    rows = exchanged(packed, devices)
    other_share = across_cores(share)
    served = expert_stage(rows, first, second)
    result = exchanged(served, devices)
    own, other = combine(lanes, share, other_share, resid, result)
    own = moved(own, lambda s, i: (s + 1, i))
    got = moved(other, lambda s, i: (s, i) if s % 2 else (s + 2, i))
    other = jnp.where(odd, other, got)
    return (own.astype(F32) + other.astype(F32)).astype(BF16)[None]


def solution(mesh):
    in_specs = (
        P("section", "expert", None),
        P("section", None, "expert"),
        P("section", "expert", None),
        P("section", "expert", None),
        P("section", "expert", None),
        P("section", "expert", None),
        P("section", None, None),
        P("section", None, "expert"),
        P("section", None, "expert"),
        P("section", "expert", None),
    )
    out_specs = P("section", "expert", None)
    return jax.shard_map(
        shards, mesh=mesh, in_specs=in_specs, out_specs=out_specs, check_vma=False
    )
```

```python
import functools

import jax
import jax.numpy as jnp
from jax import lax
from jax.experimental import pallas as pl
from jax.experimental.pallas import tpu as pltpu
from jax.sharding import PartitionSpec as P


HEADS = 8
RING = (0, 1, 2, 3, 4, -1, -2, -3)
F32 = jnp.float32
BF16 = jnp.bfloat16
VMEM = pltpu.VMEM
SMEM = pltpu.SMEM


def iota(shape, axis):
    return lax.broadcasted_iota(jnp.int32, shape, axis)


def dot(a, b):
    return jnp.dot(a, b, preferred_element_type=F32)


def dot_t(a, b):
    return lax.dot_general(a, b, (((1,), (1,)), ((), ())), preferred_element_type=F32)


def flag(mask):
    return jnp.where(mask, 1.0, 0.0).astype(BF16)


def whole(space=VMEM):
    return pl.BlockSpec(memory_space=space)


def pack_pages_body(map_ref, proj_ref, rows_hbm, out_hbm, rows_ref, out_ref, pick_ref, sems):
    count, width = rows_ref.shape
    block = width // 5
    half = block // 2
    slots = out_ref.shape[0]
    side = len(RING)
    incoming = []
    for index in range(5):
        part = pl.ds(index * block, block)
        incoming.append(
            pltpu.make_async_copy(rows_hbm.at[:, part], rows_ref.at[:, part], sems.at[index])
        )
        incoming[-1].start()
    lanes = proj_ref.shape[1] // side
    for place in range(side):
        columns = slice(place * lanes, (place + 1) * lanes)
        for part in range(2):
            piece = proj_ref[8 * part : 8 * part + 8, columns].astype(F32)
            tall = jnp.concatenate([piece] * side, axis=0).astype(BF16)
            start = 5 * half + part * lanes
            out_ref[place * 8 * side : (place + 1) * 8 * side, start : start + lanes] = tall
    outgoing = []

    def send(start, size):
        part = pl.ds(start, size)
        sem = sems.at[5 + len(outgoing)]
        outgoing.append(pltpu.make_async_copy(out_ref.at[:, part], out_hbm.at[:, part], sem))
        outgoing[-1].start()

    send(5 * half, 2 * lanes)
    device = lax.shift_right_logical(map_ref[0, 0:1, :], 5).astype(F32)
    pages = device.shape[1]
    spread = flag(iota((pages, count), 0) == lax.shift_right_logical(iota((pages, count), 1), 2))
    target = dot(jnp.broadcast_to(device, (8, pages)).astype(BF16), spread)[0:1]
    slot = iota((slots, count), 0)
    row = iota((slots, count), 1)
    hit = (lax.shift_right_logical(slot, 3) == target.astype(jnp.int32)) & ((slot & 3) == (row & 3))
    pick_ref[:, :count] = flag(hit & ((slot & 4) == 0))
    pick_ref[:, count:] = flag(hit & ((slot & 4) == 4))
    for index in range(5):
        incoming[index].wait()
        start = index * block
        both = jnp.concatenate(
            [rows_ref[:, start : start + half], rows_ref[:, start + half : start + block]], axis=0
        )
        out_ref[:, index * half : (index + 1) * half] = dot(pick_ref[...], both).astype(BF16)
        send(index * half, half)
    for copy in outgoing:
        copy.wait()


def pack_pages(page_map, proj, rows, devices):
    count, width = rows.shape
    slots = devices * 8
    wide = width // 2 + 2 * (proj.shape[1] // len(RING))
    return pl.pallas_call(
        pack_pages_body,
        name="pack_pages",
        in_specs=[whole(), whole(), whole(pl.ANY)],
        out_specs=whole(pl.ANY),
        out_shape=jax.ShapeDtypeStruct((slots, wide), BF16),
        scratch_shapes=[
            pltpu.VMEM((count, width), BF16),
            pltpu.VMEM((slots, wide), BF16),
            pltpu.VMEM((slots, 2 * count), BF16),
            pltpu.SemaphoreType.DMA((11,)),
        ],
        cost_estimate=pl.CostEstimate(flops=1 << 30, bytes_accessed=4 << 20, transcendentals=0),
    )(page_map, proj, rows)


def user_layout(index, pages_ref, tails_ref):
    users = pages_ref.shape[2]
    owner = jnp.zeros_like(index)
    offset = jnp.zeros_like(index)
    length = jnp.zeros_like(index) + ((pages_ref[0, 0, 0] - 1) * 4 + tails_ref[0, 0, 0])
    start = 0
    for user in range(1, users):
        start = start + pages_ref[0, 0, user - 1] * 4
        inside = index >= start
        owner = jnp.where(inside, user, owner)
        offset = jnp.where(inside, start, offset)
        length = jnp.where(inside, (pages_ref[0, 0, user] - 1) * 4 + tails_ref[0, 0, user], length)
    return owner, offset, length


def token_body(
    pages_ref,
    tails_ref,
    map_ref,
    routes_ref,
    router_ref,
    place_ref,
    arrived_hbm,
    *refs,
):
    proj_hbm = refs[: len(RING)]
    normed_ref, resid_ref, share_ref, arrived_ref, proj_ref, mixed_ref, sems = refs[len(RING) :]
    count, model_width = resid_ref.shape
    slots = arrived_ref.shape[0]
    half = model_width // 2
    pages = map_ref.shape[2]
    head_dim = model_width // HEADS
    copies = []
    for index in range(5):
        part = pl.ds(index * half, half)
        copies.append(
            pltpu.make_async_copy(arrived_hbm.at[:, part], arrived_ref.at[:, part], sems.at[index])
        )
    for index, shift in enumerate(RING):
        lanes = proj_hbm[index].shape[1] // 2
        start = pl.multiple_of(((place_ref[0] - shift) & (len(RING) - 1)) * lanes, lanes)
        for part in range(2):
            origin = proj_hbm[index].at[:, pl.ds(part * lanes, lanes)]
            target = proj_ref.at[pl.ds(part * slots, slots), pl.ds(start, lanes)]
            sem = sems.at[5 + 2 * index + part]
            copies.append(pltpu.make_async_copy(origin, target, sem))
    for copy in copies:
        copy.start()

    source = lax.shift_right_logical(map_ref[0, 1:2, :], 5).astype(F32)
    mine = lax.shift_right_logical(iota((count, pages), 0), 2) == iota((count, pages), 1)
    source = jnp.sum(jnp.where(mine, source, 0.0), axis=1, keepdims=True).astype(jnp.int32)
    slot = iota((count, slots), 1)
    near = lax.shift_right_logical(slot, 3) == source
    row = iota((count, slots), 0) & 3
    picks = [flag(near & ((slot & 7) == row + 4 * side)) for side in range(2)]

    def block(index, side):
        if side == 0:
            copies[index].wait()
        return dot(picks[side], arrived_ref[:, index * half : (index + 1) * half])

    rows = iota((count, count), 0)
    keys = iota((count, count), 1)
    row_owner, _, row_length = user_layout(rows, pages_ref, tails_ref)
    key_owner, key_offset, key_length = user_layout(keys, pages_ref, tails_ref)
    allowed = (row_owner == key_owner) & (keys <= rows) & (keys - key_offset < key_length)
    factor = jnp.where(allowed, 1.0 / row_length.astype(F32), 0.0)
    attended = []
    blocks = [[block(index, side).astype(BF16) for side in range(2)] for index in range(3)]
    for side in range(2):
        queries, key_rows, values = [blocks[index][side] for index in range(3)]
        for head in range(HEADS // 2):
            part = slice(head * head_dim, (head + 1) * head_dim)
            scores = dot_t(queries[:, part], key_rows[:, part]) * head_dim ** (-0.5)
            weights = (scores * jax.nn.sigmoid(scores) * factor).astype(BF16)
            attended.append(dot(weights, values[:, part]))
    total = functools.reduce(jnp.add, attended)
    average = jnp.sum(total, axis=1, keepdims=True) * (1.0 / model_width)
    attended = [part - average for part in attended]
    squares = functools.reduce(jnp.add, [part * part for part in attended])
    variance = jnp.sum(squares, axis=1, keepdims=True) * (1.0 / model_width)
    scale = lax.rsqrt(variance + 1e-05)
    wide = 2 * head_dim
    come, go = iota((wide, wide), 0), iota((wide, wide), 1)
    order = (come >> 4) * 8 + (come & 7) + ((come >> 3) & 1) * head_dim
    order = flag(order == go)
    for side in range(2):
        gating = block(3, side)
        for pair in range(HEADS // 4):
            heads = []
            for head in (2 * pair, 2 * pair + 1):
                part = slice(head * head_dim, (head + 1) * head_dim)
                mixed = attended[side * (HEADS // 2) + head] * scale * gating[:, part]
                heads.append(mixed.astype(BF16))
            sorted_pair = dot(jnp.concatenate(heads, axis=1), order).astype(BF16)
            start = (side * (HEADS // 4) + pair) * head_dim
            mixed_ref[:, start : start + head_dim] = sorted_pair[:, :head_dim]
            start += half
            mixed_ref[:, start : start + head_dim] = sorted_pair[:, head_dim:]

    squares = jnp.zeros((count, 1), F32)
    chunk = half // 2
    for side in range(2):
        inputs = block(4, side)
        if side == 0:
            for copy in copies[5:]:
                copy.wait()
        for quarter in range(2):
            part = slice(side * half + quarter * chunk, side * half + (quarter + 1) * chunk)
            projected = dot(mixed_ref[...], proj_ref[:, part])
            resid = (inputs[:, quarter * chunk : (quarter + 1) * chunk] + projected).astype(BF16)
            resid_ref[:, part] = resid
            wide = resid.astype(F32)
            squares += jnp.sum(wide * wide, axis=1, keepdims=True)
    scale = lax.rsqrt(squares * (1.0 / model_width) + 1e-06)
    for quarter in range(4):
        part = slice(quarter * chunk, (quarter + 1) * chunk)
        normed_ref[:, part] = (resid_ref[:, part].astype(F32) * scale).astype(BF16)

    experts = router_ref.shape[0]
    scores = jax.nn.sigmoid(dot_t(router_ref[...], normed_ref[...]))
    expert = iota((experts, count), 0)
    chosen = [
        jnp.sum(jnp.where(expert == routes_ref[k : k + 1, :], scores, 0.0), axis=0, keepdims=True)
        for k in range(2)
    ]
    share_ref[...] = jnp.zeros(share_ref.shape, F32)
    for k in range(2):
        share_ref[k : k + 1, :] = chosen[k] / (chosen[0] + chosen[1])


def token_stage(user_pages, tails, page_map, routes, router, place, arrived, proj, count):
    slots, wide = proj[0].shape
    width = wide // 2 * len(RING)
    return pl.pallas_call(
        token_body,
        name="token_stage",
        in_specs=[whole(SMEM)] * 2 + [whole()] * 3 + [whole(SMEM)] + [whole(pl.ANY)] * (1 + len(RING)),
        out_specs=[whole()] * 3,
        out_shape=[
            jax.ShapeDtypeStruct((count, width), BF16),
            jax.ShapeDtypeStruct((count, width), BF16),
            jax.ShapeDtypeStruct((8, count), F32),
        ],
        scratch_shapes=[
            pltpu.VMEM((slots, 5 * width // 2), BF16),
            pltpu.VMEM((2 * slots, width), BF16),
            pltpu.VMEM((count, width), BF16),
            pltpu.SemaphoreType.DMA((5 + 2 * len(RING),)),
        ],
        compiler_params=pltpu.CompilerParams(vmem_limit_bytes=40 << 20),
        cost_estimate=pl.CostEstimate(flops=2 << 30, bytes_accessed=6 << 20, transcendentals=0),
    )(user_pages, tails, page_map, routes, router, place, arrived, *proj)


def slots_body(experts, core_ref, mine_ref, theirs_ref, pick_ref, lanes_ref):
    count = mine_ref.shape[1]
    core = core_ref[0]
    capacity = 4 * count // experts
    expert = iota((experts, count), 0)
    earlier = flag(iota((count, count), 0) < iota((count, count), 1))
    row = iota((pick_ref.shape[0], count), 0)
    lanes_ref[...] = jnp.zeros(lanes_ref.shape, F32)
    for side, routes_ref in enumerate((mine_ref, theirs_ref)):
        chosen = [routes_ref[k : k + 1, :] for k in range(2)]
        named = [expert == chosen[k] for k in range(2)]
        before = dot(flag(named[0] | named[1]), earlier)
        lanes = []
        for k in range(2):
            rank = jnp.sum(jnp.where(named[k], before, 0.0), axis=0, keepdims=True)
            slot = chosen[k] * capacity + rank.astype(jnp.int32)
            half = lax.shift_right_logical(slot, 3) & 1
            lanes.append(jnp.where(half == core, slot ^ (8 * side), -1))
            lanes_ref[2 * side + k : 2 * side + k + 1, :] = lanes[k].astype(F32)
        pick_ref[:, side * count : (side + 1) * count] = flag((row == lanes[0]) | (row == lanes[1]))


def slot_tables(core, mine, theirs, experts):
    count = mine.shape[1]
    rows = 4 * count
    return pl.pallas_call(
        functools.partial(slots_body, experts),
        name="slot_tables",
        in_specs=[whole(SMEM), whole(), whole()],
        out_specs=[whole()] * 2,
        out_shape=[
            jax.ShapeDtypeStruct((rows, 2 * count), BF16),
            jax.ShapeDtypeStruct((8, count), F32),
        ],
        compiler_params=pltpu.CompilerParams(vmem_limit_bytes=4 << 20),
        cost_estimate=pl.CostEstimate(flops=1 << 24, bytes_accessed=1 << 18, transcendentals=0),
    )(core, mine, theirs)


def pack_rows_body(pick_ref, mine_ref, theirs_hbm, out_ref, theirs_ref, sem):
    copy = pltpu.make_async_copy(theirs_hbm, theirs_ref, sem)
    copy.start()
    copy.wait()
    _, width = mine_ref.shape
    chunk = width // 4
    for quarter in range(4):
        part = slice(quarter * chunk, (quarter + 1) * chunk)
        rows = jnp.concatenate([mine_ref[:, part], theirs_ref[:, part]], axis=0)
        out_ref[:, part] = dot(pick_ref[...], rows).astype(BF16)


def pack_rows(pick, mine, theirs):
    return pl.pallas_call(
        pack_rows_body,
        name="pack_rows",
        in_specs=[whole(), whole(), whole(pl.ANY)],
        out_specs=whole(),
        out_shape=jax.ShapeDtypeStruct((pick.shape[0], mine.shape[1]), BF16),
        scratch_shapes=[pltpu.VMEM(theirs.shape, BF16), pltpu.SemaphoreType.DMA],
        compiler_params=pltpu.CompilerParams(vmem_limit_bytes=4 << 20),
        cost_estimate=pl.CostEstimate(flops=1 << 28, bytes_accessed=2 << 20, transcendentals=0),
    )(pick, mine, theirs)


def expert_body(rows_hbm, *refs):
    weights_hbm = (refs[0:3], refs[3:6])
    out_hbm, out_ref, rows_ref, gate_ref, up_ref, down_ref, hidden_ref, sems = refs[6:]
    units = hidden_ref.shape[1]
    chunk = units // 2
    width = out_ref.shape[1]
    rows_copy = pltpu.make_async_copy(rows_hbm, rows_ref, sems.at[0])
    rows_copy.start()
    copies = []
    for half in range(2):
        gate_hbm, up_hbm, down_hbm = weights_hbm[half]
        for piece in range(2):
            part = pl.ds(piece * chunk, chunk)
            for hbm, ref in ((gate_hbm, gate_ref), (up_hbm, up_ref)):
                sem = sems.at[1 + len(copies)]
                copies.append(pltpu.make_async_copy(hbm.at[:, part], ref.at[half, :, part], sem))
        sem = sems.at[1 + len(copies)]
        copies.append(pltpu.make_async_copy(down_hbm, down_ref.at[half], sem))
    copies[0].start()
    copies[1].start()
    rows_copy.wait()
    for copy in copies[2:]:
        copy.start()
    pending = iter(copies)
    sent = []
    for half in range(2):
        for piece in range(2):
            part = slice(piece * chunk, (piece + 1) * chunk)
            next(pending).wait()
            gate = dot(rows_ref[...], gate_ref[half, :, part])
            next(pending).wait()
            hidden = gate * jax.nn.sigmoid(gate) * dot(rows_ref[...], up_ref[half, :, part])
            hidden_ref[:, part] = hidden.astype(BF16)
        next(pending).wait()
        for quarter in range(4):
            part = slice(quarter * width // 4, (quarter + 1) * width // 4)
            result = dot(hidden_ref[...], down_ref[half, :, part]).astype(BF16)
            if half == 1:
                result = (out_ref[:, part].astype(F32) + result.astype(F32)).astype(BF16)
            out_ref[:, part] = result
            if half == 1:
                part = pl.ds(quarter * width // 4, width // 4)
                sem = sems.at[11 + quarter]
                sent.append(pltpu.make_async_copy(out_ref.at[:, part], out_hbm.at[:, part], sem))
                sent[-1].start()
    for copy in sent:
        copy.wait()


def expert_stage(rows, first, second):
    count, width = rows.shape
    units = first[0].shape[1]
    return pl.pallas_call(
        expert_body,
        name="expert_stage",
        in_specs=[whole(pl.ANY)] * 7,
        out_specs=whole(pl.ANY),
        out_shape=jax.ShapeDtypeStruct((count, width), BF16),
        scratch_shapes=[
            pltpu.VMEM((count, width), BF16),
            pltpu.VMEM((count, width), BF16),
            pltpu.VMEM((2, width, units), BF16),
            pltpu.VMEM((2, width, units), BF16),
            pltpu.VMEM((2, units, width), BF16),
            pltpu.VMEM((count, units), BF16),
            pltpu.SemaphoreType.DMA((15,)),
        ],
        compiler_params=pltpu.CompilerParams(vmem_limit_bytes=50 << 20),
        cost_estimate=pl.CostEstimate(flops=4 << 30, bytes_accessed=8 << 20, transcendentals=0),
    )(rows, *first, *second)


def combine_body(
    lanes_ref, mine_ref, theirs_ref, resid_ref, rows_hbm, own_ref, other_ref, rows_ref, sem
):
    copy = pltpu.make_async_copy(rows_hbm, rows_ref, sem)
    copy.start()
    count, width = resid_ref.shape
    slots = rows_ref.shape[0]
    table = jnp.concatenate([lanes_ref[0:4, :], mine_ref[0:2, :], theirs_ref[0:2, :]], axis=0)
    table = jnp.transpose(table)
    slot = iota((count, slots), 1).astype(F32)
    shares = []
    for side in range(2):
        share = jnp.zeros((count, slots), F32)
        for k in range(2):
            lane = 2 * side + k
            share += jnp.where(slot == table[:, lane : lane + 1], table[:, 4 + lane : 5 + lane], 0.0)
        high = share.astype(BF16)
        shares.append((high, (share - high.astype(F32)).astype(BF16)))
    chunk = width // 4
    copy.wait()
    for quarter in range(4):
        part = slice(quarter * chunk, (quarter + 1) * chunk)
        rows = rows_ref[:, part]
        own, other = [dot(high, rows) + dot(low, rows) for high, low in shares]
        own_ref[:, part] = (resid_ref[:, part].astype(F32) + own).astype(BF16)
        other_ref[:, part] = other.astype(BF16)


def combine(lanes, mine, theirs, resid, rows):
    return pl.pallas_call(
        combine_body,
        name="combine",
        in_specs=[whole()] * 4 + [whole(pl.ANY)],
        out_specs=[whole()] * 2,
        out_shape=[jax.ShapeDtypeStruct(resid.shape, BF16)] * 2,
        scratch_shapes=[pltpu.VMEM(rows.shape, BF16), pltpu.SemaphoreType.DMA],
        compiler_params=pltpu.CompilerParams(vmem_limit_bytes=10 << 20),
        cost_estimate=pl.CostEstimate(flops=1 << 29, bytes_accessed=2 << 20, transcendentals=0),
    )(lanes, mine, theirs, resid, rows)


def moved(shard, where):
    sections, devices = lax.axis_size("section"), lax.axis_size("expert")
    route = []
    for s in range(sections):
        for i in range(devices):
            to_s, to_i = where(s, i)
            if (to_s, to_i) != (s, i):
                route.append((s * devices + i, to_s % sections * devices + to_i))
    return lax.ppermute(shard, ("section", "expert"), route)


def across_cores(shard):
    return moved(shard, lambda s, i: (s ^ 1, i))


def exchanged(blocks, devices):
    rows, width = blocks.shape
    sent = blocks.reshape(devices, rows // devices, width)
    return lax.all_to_all(sent, "expert", split_axis=0, concat_axis=0, tiled=True).reshape(rows, width)


def shifted(shard, apart):
    size = lax.axis_size("expert")
    return lax.ppermute(shard, "expert", [(i, (i + apart) % size) for i in range(size)])


def ringed(block):
    side = len(RING)
    blocks = {0: block}
    for step in range(1, side // 2 + 1):
        blocks[step] = shifted(blocks[step - 1], side)
        if step < side // 2:
            blocks[-step] = shifted(blocks[1 - step], -side)
    return [blocks[shift] for shift in RING]


def shards(histories, page_map, user_pages, tails, routes, out_proj, router, w_gate, w_up, w_down):
    devices = lax.axis_size("expert")
    count = histories.shape[1]
    experts = router.shape[2]
    weights = dict(gate=w_gate[0], up=w_up[0], down=w_down[0])
    mine = routes[0].T
    outgoing = pack_pages(page_map, out_proj[0], histories[0], devices)
    arrived = exchanged(outgoing, devices)
    block = arrived[:, histories.shape[2] // 2 :]
    weights = dict(zip(weights, lax.optimization_barrier((*weights.values(), block))))
    first, second = [], []
    odd = (lax.axis_index("section") & 1) == 1
    trader = odd != ((lax.axis_index("expert") & 1) == 1)
    for weight in weights.values():
        got = moved(weight, lambda s, i: (s, i) if s % 2 == i % 2 else (s ^ 1, i ^ 1))
        first.append(jnp.where(trader, got, weight))
        second.append(across_cores(first[-1]))
    proj = ringed(block)
    theirs = across_cores(mine)
    core = (lax.axis_index("section") & 1).astype(jnp.int32).reshape(1)
    place = lax.shift_right_logical(lax.axis_index("expert"), 3).astype(jnp.int32).reshape(1)
    pick, lanes = slot_tables(core, mine, theirs, experts)
    normed, resid, share = token_stage(
        user_pages, tails, page_map, mine, router[0].T, place, arrived, proj, count
    )
    other_rows = across_cores(normed)
    packed = pack_rows(pick, normed, other_rows)
    rows = exchanged(packed, devices)
    other_share = across_cores(share)
    served = expert_stage(rows, first, second)
    result = exchanged(served, devices)
    own, other = combine(lanes, share, other_share, resid, result)
    own = moved(own, lambda s, i: (s + 1, i))
    got = moved(other, lambda s, i: (s, i) if s % 2 else (s + 2, i))
    other = jnp.where(odd, other, got)
    return (own.astype(F32) + other.astype(F32)).astype(BF16)[None]


def solution(mesh):
    in_specs = (
        P("section", "expert", None),
        P("section", None, "expert"),
        P("section", "expert", None),
        P("section", "expert", None),
        P("section", "expert", None),
        P("section", "expert", None),
        P("section", None, None),
        P("section", None, "expert"),
        P("section", None, "expert"),
        P("section", "expert", None),
    )
    out_specs = P("section", "expert", None)
    return jax.shard_map(
        shards, mesh=mesh, in_specs=in_specs, out_specs=out_specs, check_vma=False
    )
```

```python
import functools

import jax
import jax.numpy as jnp
from jax import lax
from jax.experimental import pallas as pl
from jax.experimental.pallas import tpu as pltpu
from jax.sharding import PartitionSpec as P


HEADS = 8
RING = (0, 1, 2, 3, 4, -1, -2, -3)
F32 = jnp.float32
BF16 = jnp.bfloat16
VMEM = pltpu.VMEM
SMEM = pltpu.SMEM


def iota(shape, axis):
    return lax.broadcasted_iota(jnp.int32, shape, axis)


def dot(a, b):
    return jnp.dot(a, b, preferred_element_type=F32)


def dot_t(a, b):
    return lax.dot_general(a, b, (((1,), (1,)), ((), ())), preferred_element_type=F32)


def flag(mask):
    return jnp.where(mask, 1.0, 0.0).astype(BF16)


def whole(space=VMEM):
    return pl.BlockSpec(memory_space=space)


def pack_pages_body(map_ref, rows_hbm, out_hbm, rows_ref, out_ref, pick_ref, sems):
    count, width = rows_ref.shape
    block = width // 5
    half = block // 2
    slots = out_ref.shape[0]
    incoming, outgoing = [], []
    for index in range(5):
        part = pl.ds(index * block, block)
        incoming.append(
            pltpu.make_async_copy(rows_hbm.at[:, part], rows_ref.at[:, part], sems.at[index])
        )
        incoming[-1].start()
    device = lax.shift_right_logical(map_ref[0, 0:1, :], 5).astype(F32)
    pages = device.shape[1]
    spread = flag(iota((pages, count), 0) == lax.shift_right_logical(iota((pages, count), 1), 2))
    target = dot(jnp.broadcast_to(device, (8, pages)).astype(BF16), spread)[0:1]
    slot = iota((slots, count), 0)
    row = iota((slots, count), 1)
    hit = (lax.shift_right_logical(slot, 3) == target.astype(jnp.int32)) & ((slot & 3) == (row & 3))
    pick_ref[:, :count] = flag(hit & ((slot & 4) == 0))
    pick_ref[:, count:] = flag(hit & ((slot & 4) == 4))
    for index in range(5):
        incoming[index].wait()
        start = index * block
        both = jnp.concatenate(
            [rows_ref[:, start : start + half], rows_ref[:, start + half : start + block]], axis=0
        )
        out_ref[:, index * half : (index + 1) * half] = dot(pick_ref[...], both).astype(BF16)
        part = pl.ds(index * half, half)
        outgoing.append(
            pltpu.make_async_copy(out_ref.at[:, part], out_hbm.at[:, part], sems.at[5 + index])
        )
        outgoing[-1].start()
    for copy in outgoing:
        copy.wait()


def pack_pages(page_map, rows, devices):
    count, width = rows.shape
    slots = devices * 8
    return pl.pallas_call(
        pack_pages_body,
        name="pack_pages",
        in_specs=[whole(), whole(pl.ANY)],
        out_specs=whole(pl.ANY),
        out_shape=jax.ShapeDtypeStruct((slots, width // 2), BF16),
        scratch_shapes=[
            pltpu.VMEM((count, width), BF16),
            pltpu.VMEM((slots, width // 2), BF16),
            pltpu.VMEM((slots, 2 * count), BF16),
            pltpu.SemaphoreType.DMA((10,)),
        ],
        cost_estimate=pl.CostEstimate(flops=1 << 30, bytes_accessed=4 << 20, transcendentals=0),
    )(page_map, rows)


def user_layout(index, pages_ref, tails_ref):
    users = pages_ref.shape[2]
    owner = jnp.zeros_like(index)
    offset = jnp.zeros_like(index)
    length = jnp.zeros_like(index) + ((pages_ref[0, 0, 0] - 1) * 4 + tails_ref[0, 0, 0])
    start = 0
    for user in range(1, users):
        start = start + pages_ref[0, 0, user - 1] * 4
        inside = index >= start
        owner = jnp.where(inside, user, owner)
        offset = jnp.where(inside, start, offset)
        length = jnp.where(inside, (pages_ref[0, 0, user] - 1) * 4 + tails_ref[0, 0, user], length)
    return owner, offset, length


def token_body(
    pages_ref,
    tails_ref,
    map_ref,
    routes_ref,
    router_ref,
    place_ref,
    arrived_hbm,
    *refs,
):
    proj_hbm = refs[: len(RING)]
    normed_ref, resid_ref, share_ref, arrived_ref, proj_ref, mixed_ref, sems = refs[len(RING) :]
    count, model_width = resid_ref.shape
    slots = arrived_ref.shape[0]
    half = arrived_ref.shape[1] // 5
    pages = map_ref.shape[2]
    head_dim = model_width // HEADS
    copies = []
    for index in range(5):
        part = pl.ds(index * half, half)
        copies.append(
            pltpu.make_async_copy(arrived_hbm.at[:, part], arrived_ref.at[:, part], sems.at[index])
        )
    for index, shift in enumerate(RING):
        rows = proj_hbm[index].shape[0]
        start = pl.multiple_of(((place_ref[0] - shift) & (len(RING) - 1)) * rows, rows)
        target = proj_ref.at[pl.ds(start, rows)]
        copies.append(pltpu.make_async_copy(proj_hbm[index], target, sems.at[5 + index]))
    for copy in copies:
        copy.start()

    source = lax.shift_right_logical(map_ref[0, 1:2, :], 5).astype(F32)
    mine = lax.shift_right_logical(iota((count, pages), 0), 2) == iota((count, pages), 1)
    source = jnp.sum(jnp.where(mine, source, 0.0), axis=1, keepdims=True).astype(jnp.int32)
    slot = iota((count, slots), 1)
    near = lax.shift_right_logical(slot, 3) == source
    row = iota((count, slots), 0) & 3
    picks = [flag(near & ((slot & 7) == row + 4 * side)) for side in range(2)]

    def block(index, side):
        if side == 0:
            copies[index].wait()
        return dot(picks[side], arrived_ref[:, index * half : (index + 1) * half])

    rows = iota((count, count), 0)
    keys = iota((count, count), 1)
    row_owner, _, row_length = user_layout(rows, pages_ref, tails_ref)
    key_owner, key_offset, key_length = user_layout(keys, pages_ref, tails_ref)
    allowed = (row_owner == key_owner) & (keys <= rows) & (keys - key_offset < key_length)
    factor = jnp.where(allowed, 1.0 / row_length.astype(F32), 0.0)
    attended = []
    blocks = [[block(index, side).astype(BF16) for side in range(2)] for index in range(3)]
    for side in range(2):
        queries, key_rows, values = [blocks[index][side] for index in range(3)]
        for head in range(HEADS // 2):
            part = slice(head * head_dim, (head + 1) * head_dim)
            scores = dot_t(queries[:, part], key_rows[:, part]) * head_dim ** (-0.5)
            weights = (scores * jax.nn.sigmoid(scores) * factor).astype(BF16)
            attended.append(dot(weights, values[:, part]))
    total = functools.reduce(jnp.add, attended)
    average = jnp.sum(total, axis=1, keepdims=True) * (1.0 / model_width)
    attended = [part - average for part in attended]
    squares = functools.reduce(jnp.add, [part * part for part in attended])
    variance = jnp.sum(squares, axis=1, keepdims=True) * (1.0 / model_width)
    scale = lax.rsqrt(variance + 1e-05)
    for side in range(2):
        gating = block(3, side)
        for head in range(HEADS // 2):
            part = slice(head * head_dim, (head + 1) * head_dim)
            index = side * (HEADS // 2) + head
            mixed = attended[index] * scale * gating[:, part]
            mixed_ref[:, index * head_dim : (index + 1) * head_dim] = mixed.astype(BF16)

    squares = jnp.zeros((count, 1), F32)
    chunk = half // 2
    for side in range(2):
        inputs = block(4, side)
        if side == 0:
            for copy in copies[5:]:
                copy.wait()
        for quarter in range(2):
            part = slice(side * half + quarter * chunk, side * half + (quarter + 1) * chunk)
            projected = dot(mixed_ref[...], proj_ref[:, part])
            resid = (inputs[:, quarter * chunk : (quarter + 1) * chunk] + projected).astype(BF16)
            resid_ref[:, part] = resid
            wide = resid.astype(F32)
            squares += jnp.sum(wide * wide, axis=1, keepdims=True)
    scale = lax.rsqrt(squares * (1.0 / model_width) + 1e-06)
    for quarter in range(4):
        part = slice(quarter * chunk, (quarter + 1) * chunk)
        normed_ref[:, part] = (resid_ref[:, part].astype(F32) * scale).astype(BF16)

    experts = router_ref.shape[0]
    scores = jax.nn.sigmoid(dot_t(router_ref[...], normed_ref[...]))
    expert = iota((experts, count), 0)
    chosen = [
        jnp.sum(jnp.where(expert == routes_ref[k : k + 1, :], scores, 0.0), axis=0, keepdims=True)
        for k in range(2)
    ]
    share_ref[...] = jnp.zeros(share_ref.shape, F32)
    for k in range(2):
        share_ref[k : k + 1, :] = chosen[k] / (chosen[0] + chosen[1])


def token_stage(user_pages, tails, page_map, routes, router, place, arrived, proj, count):
    depth, width = proj[0].shape
    return pl.pallas_call(
        token_body,
        name="token_stage",
        in_specs=[whole(SMEM)] * 2 + [whole()] * 3 + [whole(SMEM)] + [whole(pl.ANY)] * (1 + len(RING)),
        out_specs=[whole()] * 3,
        out_shape=[
            jax.ShapeDtypeStruct((count, width), BF16),
            jax.ShapeDtypeStruct((count, width), BF16),
            jax.ShapeDtypeStruct((8, count), F32),
        ],
        scratch_shapes=[
            pltpu.VMEM(arrived.shape, BF16),
            pltpu.VMEM((depth * len(RING), width), BF16),
            pltpu.VMEM((count, width), BF16),
            pltpu.SemaphoreType.DMA((5 + len(RING),)),
        ],
        compiler_params=pltpu.CompilerParams(vmem_limit_bytes=40 << 20),
        cost_estimate=pl.CostEstimate(flops=2 << 30, bytes_accessed=6 << 20, transcendentals=0),
    )(user_pages, tails, page_map, routes, router, place, arrived, *proj)


def slots_body(experts, core_ref, mine_ref, theirs_ref, pick_ref, lanes_ref):
    count = mine_ref.shape[1]
    core = core_ref[0]
    capacity = 4 * count // experts
    expert = iota((experts, count), 0)
    earlier = flag(iota((count, count), 0) < iota((count, count), 1))
    row = iota((pick_ref.shape[0], count), 0)
    lanes_ref[...] = jnp.zeros(lanes_ref.shape, F32)
    for side, routes_ref in enumerate((mine_ref, theirs_ref)):
        chosen = [routes_ref[k : k + 1, :] for k in range(2)]
        named = [expert == chosen[k] for k in range(2)]
        before = dot(flag(named[0] | named[1]), earlier)
        lanes = []
        for k in range(2):
            rank = jnp.sum(jnp.where(named[k], before, 0.0), axis=0, keepdims=True)
            slot = chosen[k] * capacity + rank.astype(jnp.int32)
            half = lax.shift_right_logical(slot, 3) & 1
            lanes.append(jnp.where(half == core, slot ^ (8 * side), -1))
            lanes_ref[2 * side + k : 2 * side + k + 1, :] = lanes[k].astype(F32)
        pick_ref[:, side * count : (side + 1) * count] = flag((row == lanes[0]) | (row == lanes[1]))


def slot_tables(core, mine, theirs, experts):
    count = mine.shape[1]
    rows = 4 * count
    return pl.pallas_call(
        functools.partial(slots_body, experts),
        name="slot_tables",
        in_specs=[whole(SMEM), whole(), whole()],
        out_specs=[whole()] * 2,
        out_shape=[
            jax.ShapeDtypeStruct((rows, 2 * count), BF16),
            jax.ShapeDtypeStruct((8, count), F32),
        ],
        compiler_params=pltpu.CompilerParams(vmem_limit_bytes=4 << 20),
        cost_estimate=pl.CostEstimate(flops=1 << 24, bytes_accessed=1 << 18, transcendentals=0),
    )(core, mine, theirs)


def pack_rows_body(pick_ref, mine_ref, theirs_hbm, out_ref, theirs_ref, sem):
    copy = pltpu.make_async_copy(theirs_hbm, theirs_ref, sem)
    copy.start()
    copy.wait()
    _, width = mine_ref.shape
    chunk = width // 4
    for quarter in range(4):
        part = slice(quarter * chunk, (quarter + 1) * chunk)
        rows = jnp.concatenate([mine_ref[:, part], theirs_ref[:, part]], axis=0)
        out_ref[:, part] = dot(pick_ref[...], rows).astype(BF16)


def pack_rows(pick, mine, theirs):
    return pl.pallas_call(
        pack_rows_body,
        name="pack_rows",
        in_specs=[whole(), whole(), whole(pl.ANY)],
        out_specs=whole(),
        out_shape=jax.ShapeDtypeStruct((pick.shape[0], mine.shape[1]), BF16),
        scratch_shapes=[pltpu.VMEM(theirs.shape, BF16), pltpu.SemaphoreType.DMA],
        compiler_params=pltpu.CompilerParams(vmem_limit_bytes=4 << 20),
        cost_estimate=pl.CostEstimate(flops=1 << 28, bytes_accessed=2 << 20, transcendentals=0),
    )(pick, mine, theirs)


def expert_body(rows_hbm, *refs):
    weights_hbm = (refs[0:3], refs[3:6])
    out_hbm, out_ref, rows_ref, gate_ref, up_ref, down_ref, hidden_ref, sems = refs[6:]
    units = hidden_ref.shape[1]
    chunk = units // 2
    width = out_ref.shape[1]
    rows_copy = pltpu.make_async_copy(rows_hbm, rows_ref, sems.at[0])
    rows_copy.start()
    copies = []
    for half in range(2):
        gate_hbm, up_hbm, down_hbm = weights_hbm[half]
        for piece in range(2):
            part = pl.ds(piece * chunk, chunk)
            for hbm, ref in ((gate_hbm, gate_ref), (up_hbm, up_ref)):
                sem = sems.at[1 + len(copies)]
                copies.append(pltpu.make_async_copy(hbm.at[:, part], ref.at[half, :, part], sem))
        sem = sems.at[1 + len(copies)]
        copies.append(pltpu.make_async_copy(down_hbm, down_ref.at[half], sem))
    copies[0].start()
    copies[1].start()
    rows_copy.wait()
    for copy in copies[2:]:
        copy.start()
    pending = iter(copies)
    sent = []
    for half in range(2):
        for piece in range(2):
            part = slice(piece * chunk, (piece + 1) * chunk)
            next(pending).wait()
            gate = dot(rows_ref[...], gate_ref[half, :, part])
            next(pending).wait()
            hidden = gate * jax.nn.sigmoid(gate) * dot(rows_ref[...], up_ref[half, :, part])
            hidden_ref[:, part] = hidden.astype(BF16)
        next(pending).wait()
        for quarter in range(4):
            part = slice(quarter * width // 4, (quarter + 1) * width // 4)
            result = dot(hidden_ref[...], down_ref[half, :, part]).astype(BF16)
            if half == 1:
                result = (out_ref[:, part].astype(F32) + result.astype(F32)).astype(BF16)
            out_ref[:, part] = result
            if half == 1:
                part = pl.ds(quarter * width // 4, width // 4)
                sem = sems.at[11 + quarter]
                sent.append(pltpu.make_async_copy(out_ref.at[:, part], out_hbm.at[:, part], sem))
                sent[-1].start()
    for copy in sent:
        copy.wait()


def expert_stage(rows, first, second):
    count, width = rows.shape
    units = first[0].shape[1]
    return pl.pallas_call(
        expert_body,
        name="expert_stage",
        in_specs=[whole(pl.ANY)] * 7,
        out_specs=whole(pl.ANY),
        out_shape=jax.ShapeDtypeStruct((count, width), BF16),
        scratch_shapes=[
            pltpu.VMEM((count, width), BF16),
            pltpu.VMEM((count, width), BF16),
            pltpu.VMEM((2, width, units), BF16),
            pltpu.VMEM((2, width, units), BF16),
            pltpu.VMEM((2, units, width), BF16),
            pltpu.VMEM((count, units), BF16),
            pltpu.SemaphoreType.DMA((15,)),
        ],
        compiler_params=pltpu.CompilerParams(vmem_limit_bytes=50 << 20),
        cost_estimate=pl.CostEstimate(flops=4 << 30, bytes_accessed=8 << 20, transcendentals=0),
    )(rows, *first, *second)


def combine_body(
    lanes_ref, mine_ref, theirs_ref, resid_ref, rows_hbm, own_ref, other_ref, rows_ref, sem
):
    copy = pltpu.make_async_copy(rows_hbm, rows_ref, sem)
    copy.start()
    count, width = resid_ref.shape
    slots = rows_ref.shape[0]
    table = jnp.concatenate([lanes_ref[0:4, :], mine_ref[0:2, :], theirs_ref[0:2, :]], axis=0)
    table = jnp.transpose(table)
    slot = iota((count, slots), 1).astype(F32)
    shares = []
    for side in range(2):
        share = jnp.zeros((count, slots), F32)
        for k in range(2):
            lane = 2 * side + k
            share += jnp.where(slot == table[:, lane : lane + 1], table[:, 4 + lane : 5 + lane], 0.0)
        high = share.astype(BF16)
        shares.append((high, (share - high.astype(F32)).astype(BF16)))
    chunk = width // 4
    copy.wait()
    for quarter in range(4):
        part = slice(quarter * chunk, (quarter + 1) * chunk)
        rows = rows_ref[:, part]
        own, other = [dot(high, rows) + dot(low, rows) for high, low in shares]
        own_ref[:, part] = (resid_ref[:, part].astype(F32) + own).astype(BF16)
        other_ref[:, part] = other.astype(BF16)


def combine(lanes, mine, theirs, resid, rows):
    return pl.pallas_call(
        combine_body,
        name="combine",
        in_specs=[whole()] * 4 + [whole(pl.ANY)],
        out_specs=[whole()] * 2,
        out_shape=[jax.ShapeDtypeStruct(resid.shape, BF16)] * 2,
        scratch_shapes=[pltpu.VMEM(rows.shape, BF16), pltpu.SemaphoreType.DMA],
        compiler_params=pltpu.CompilerParams(vmem_limit_bytes=10 << 20),
        cost_estimate=pl.CostEstimate(flops=1 << 29, bytes_accessed=2 << 20, transcendentals=0),
    )(lanes, mine, theirs, resid, rows)


def moved(shard, where):
    sections, devices = lax.axis_size("section"), lax.axis_size("expert")
    route = []
    for s in range(sections):
        for i in range(devices):
            to_s, to_i = where(s, i)
            if (to_s, to_i) != (s, i):
                route.append((s * devices + i, to_s % sections * devices + to_i))
    return lax.ppermute(shard, ("section", "expert"), route)


def across_cores(shard):
    return moved(shard, lambda s, i: (s ^ 1, i))


def exchanged(blocks, devices):
    rows, width = blocks.shape
    sent = blocks.reshape(devices, rows // devices, width)
    return lax.all_to_all(sent, "expert", split_axis=0, concat_axis=0, tiled=True).reshape(rows, width)


def shifted(shard, apart):
    size = lax.axis_size("expert")
    return lax.ppermute(shard, "expert", [(i, (i + apart) % size) for i in range(size)])


def column_block(piece):
    side = len(RING)
    devices = lax.axis_size("expert")
    groups = [list(range(start, start + side)) for start in range(0, devices, side)]
    copies = jnp.broadcast_to(piece[None], (side,) + piece.shape)
    block = lax.all_to_all(
        copies, "expert", split_axis=0, concat_axis=0, tiled=True, axis_index_groups=groups
    )
    return block.reshape(-1, piece.shape[1])


def ringed(block):
    side = len(RING)
    blocks = {0: block}
    for step in range(1, side // 2 + 1):
        blocks[step] = shifted(blocks[step - 1], side)
        if step < side // 2:
            blocks[-step] = shifted(blocks[1 - step], -side)
    return [blocks[shift] for shift in RING]


def shards(histories, page_map, user_pages, tails, routes, out_proj, router, w_gate, w_up, w_down):
    devices = lax.axis_size("expert")
    count = histories.shape[1]
    experts = router.shape[2]
    weights = dict(gate=w_gate[0], up=w_up[0], down=w_down[0])
    mine = routes[0].T
    block = column_block(out_proj[0])
    weights = dict(zip(weights, lax.optimization_barrier((*weights.values(), block))))
    first, second = [], []
    odd = (lax.axis_index("section") & 1) == 1
    trader = odd != ((lax.axis_index("expert") & 1) == 1)
    for weight in weights.values():
        got = moved(weight, lambda s, i: (s, i) if s % 2 == i % 2 else (s ^ 1, i ^ 1))
        first.append(jnp.where(trader, got, weight))
        second.append(across_cores(first[-1]))
    proj = ringed(block)
    outgoing = pack_pages(page_map, histories[0], devices)
    arrived = exchanged(outgoing, devices)
    theirs = across_cores(mine)
    core = (lax.axis_index("section") & 1).astype(jnp.int32).reshape(1)
    place = lax.shift_right_logical(lax.axis_index("expert"), 3).astype(jnp.int32).reshape(1)
    pick, lanes = slot_tables(core, mine, theirs, experts)
    normed, resid, share = token_stage(
        user_pages, tails, page_map, mine, router[0].T, place, arrived, proj, count
    )
    other_rows = across_cores(normed)
    packed = pack_rows(pick, normed, other_rows)
    rows = exchanged(packed, devices)
    other_share = across_cores(share)
    served = expert_stage(rows, first, second)
    result = exchanged(served, devices)
    own, other = combine(lanes, share, other_share, resid, result)
    own = moved(own, lambda s, i: (s + 1, i))
    got = moved(other, lambda s, i: (s, i) if s % 2 else (s + 2, i))
    other = jnp.where(odd, other, got)
    return (own.astype(F32) + other.astype(F32)).astype(BF16)[None]


def solution(mesh):
    in_specs = (
        P("section", "expert", None),
        P("section", None, "expert"),
        P("section", "expert", None),
        P("section", "expert", None),
        P("section", "expert", None),
        P("section", "expert", None),
        P("section", None, None),
        P("section", None, "expert"),
        P("section", None, "expert"),
        P("section", "expert", None),
    )
    out_specs = P("section", "expert", None)
    return jax.shard_map(
        shards, mesh=mesh, in_specs=in_specs, out_specs=out_specs, check_vma=False
    )
```
